32 devices in a mesh: tm: 16 (over z, y, x), col: 2 (over core).
Axes of the slice: x: 2, y: 2, z: 4, core: 2. Of those that a mesh axis runs over, the one named last changes fastest.
Arguments:
- diagonal_blocks: float32 [32, 512, 512], P('tm', 'col'), as said below
- upper_blocks: float32 [32, 512, 512], P('tm', 'col')
- right_sides: float32 [32, 512, 512], P('tm', 'col'), may hold values from -6 to 6
Outputs:
- reduced_blocks: float32 [32, 512, 512], P('tm', 'col')
- reduced_uppers: float32 [32, 512, 512], P('tm', 'col')
- reduced_sources: float32 [32, 512, 512], P('tm', 'col')
The draws below stay inside these ranges and needn't reach their ends.
Inputs may be any that keep to these rules, and one draw needn't show every extreme that they name: `diagonal_blocks`: every block is symmetric, and the block-tridiagonal matrix built from these blocks and upper_blocks is positive definite.
All inputs are finite; a program needn't handle non-finite values.
Results may differ from the reference program's by a relative error of at most 0.0001.
Values sent between devices are 32-bit elements; how exact they have to be, the bound alone decides.
A program may use at most 64 MiB of HBM per device.

```python
import jax
import jax.numpy as jnp
from jax import lax

MODES = 512
SOURCES = 512
LEVELS = 2
ROWS = 32


def coupling_factor(key):
    phi_key = jax.random.fold_in(key, 11)
    entries = jnp.clip(jax.random.normal(phi_key, (ROWS, MODES, MODES), jnp.float32), -6.0, 6.0)
    return entries * (2.0 / jnp.sqrt(1.0 * MODES))


def draw_diagonal_blocks(key, part):
    factor = coupling_factor(key)
    dense_key = jax.random.fold_in(key, 23)
    height_key = jax.random.fold_in(key, 37)
    dense = jnp.clip(jax.random.normal(dense_key, (ROWS, MODES, MODES), jnp.float32), -6.0, 6.0)
    dense = dense * (2.0 / jnp.sqrt(1.0 * MODES))
    total = jnp.einsum('nab,ncb->nac', factor, factor, precision=lax.Precision.HIGHEST) + jnp.einsum('nab,ncb->nac', dense, dense, precision=lax.Precision.HIGHEST)
    total = 0.5 * (total + jnp.swapaxes(total, 1, 2))
    heights = jnp.exp(jax.random.uniform(height_key, (ROWS, MODES), jnp.float32, jnp.log(3.0), jnp.log(9.0)))
    return total + heights[:, :, None] * jnp.eye(MODES, dtype=jnp.float32)


def draw_upper_blocks(key, part):
    return -jnp.swapaxes(coupling_factor(key), 1, 2)


def block_levels(own_key, shape, pieces, least, top_value):
    gain = 1.0
    for axis_at, parts in pieces:
        draws = jax.random.uniform(jax.random.fold_in(jax.random.fold_in(own_key, 6), axis_at), (parts,), jnp.float32, least / len(pieces), top_value / len(pieces))
        gain = gain * jnp.repeat(jnp.exp(draws), shape[axis_at] // parts).reshape((-1,) + (1,) * (len(shape) - 1 - axis_at))
    return gain


def noise(own_key, dims, width, most, pieces=(), kind=jnp.bfloat16):
    result = jax.random.normal(own_key, dims, jnp.float32) * width
    if len(pieces) > 0:
        result = block_levels(own_key, dims, pieces, -0.22, 0.18) * result
    return jnp.clip(result, min=-most, max=most).astype(kind)


def setup_inputs(seed: int = 0) -> dict:
    streams_of = jax.random.split(jax.random.key(seed), 4)
    diagonal_blocks = draw_diagonal_blocks(jax.random.fold_in(streams_of[3], 71), 0)
    upper_blocks = draw_upper_blocks(jax.random.fold_in(streams_of[3], 71), 0)
    right_sides = noise(streams_of[2], (ROWS, SOURCES, MODES), 1.0, 6.0, ((0, 16), (1, 2)), jnp.float32)
    return dict(diagonal_blocks=diagonal_blocks, upper_blocks=upper_blocks, right_sides=right_sides)


HIGHEST = lax.Precision.HIGHEST

def solve_right(factor, values, transposed):
    return lax.linalg.triangular_solve(factor, values, left_side=False, lower=True, transpose_a=transposed)

def apply_inverse(factor, values):
    return solve_right(factor, solve_right(factor, values, True), False)

def product(pattern, left_operand, right_operand):
    return jnp.einsum(pattern, left_operand, right_operand, precision=HIGHEST)

def eliminate(pivot, coupling, onward, sources):
    factor = lax.linalg.cholesky(pivot)
    scaled = apply_inverse(factor, coupling)
    solved = apply_inverse(factor, sources)
    turned = apply_inverse(factor, jnp.swapaxes(onward, 1, 2))
    left_block = -product('nab,ncb->nac', scaled, coupling)
    left_source = -product('nkb,ncb->nkc', solved, coupling)
    right_block = -product('nab,nbc->nac', turned, onward)
    right_upper = -product('nab,nbc->nac', scaled, onward)
    right_source = -product('nkb,nbc->nkc', solved, onward)
    return (left_block, left_source, right_block, right_upper, right_source)

def shifted(values):
    return jnp.concatenate([jnp.zeros_like(values[:1]), values[:-1]], axis=0)

def reference(diagonal_blocks, upper_blocks, right_sides):
    blocks = diagonal_blocks
    uppers = upper_blocks
    sources = right_sides
    for level_index in range(LEVELS):
        stride = 2 ** level_index
        active_block = blocks[::stride]
        active_upper = uppers[::stride]
        active_source = sources[::stride]
        onward = jnp.concatenate([active_upper[2::2], jnp.zeros_like(active_upper[:1])], axis=0)
        left_block, left_source, right_block, right_upper, right_source = eliminate(active_block[1::2], active_upper[1::2], onward, active_source[1::2])
        kept_block = active_block[0::2] + left_block + shifted(right_block)
        kept_upper = jnp.concatenate([active_upper[:1], right_upper[:-1]], axis=0)
        kept_source = active_source[0::2] + left_source + shifted(right_source)
        blocks = blocks.at[::2 * stride].set(kept_block)
        uppers = uppers.at[::2 * stride].set(kept_upper)
        sources = sources.at[::2 * stride].set(kept_source)
    return (blocks, uppers, sources)
```

```python
import functools

import jax
import jax.numpy as jnp
from jax import lax
from jax.experimental import pallas as pl
from jax.experimental.pallas import tpu as pltpu
from jax.sharding import PartitionSpec as P

LEVELS = 2
TILE = 128
PANEL = 8
F32 = jnp.float32
BF16 = jnp.bfloat16


def split(values):
    high = values.astype(BF16)
    return high, (values - high.astype(F32)).astype(BF16)


def dot_parts(left, right, dims):
    def one(a, b):
        return lax.dot_general(a, b, (dims, ((), ())), preferred_element_type=F32)

    return one(left[0], right[0]) + (one(left[0], right[1]) + one(left[1], right[0]))


def dot3(left, right, dims=((1,), (0,))):
    return dot_parts(split(left), split(right), dims)


def panel_step(a, p):
    size = a[0].shape[1]
    count = size // PANEL
    base = PANEL * p
    lanes = lax.broadcasted_iota(jnp.int32, (PANEL, size), 1)
    subs = lax.broadcasted_iota(jnp.int32, (PANEL, size), 0)
    inside = jnp.logical_and(lanes >= base, lanes < base + PANEL)

    def spread(values, i):
        return jnp.broadcast_to(values[:, base + i : base + i + 1], (PANEL, size))

    head = [spread(a[p], i) for i in range(PANEL)]
    s = [
        [jnp.broadcast_to(head[j][i : i + 1, :], (PANEL, size)) if j >= i else None for j in range(PANEL)]
        for i in range(PANEL)
    ]
    rows = [
        jnp.where(
            inside,
            jnp.where(lanes == base + i, 1.0, 0.0),
            jnp.broadcast_to(a[p][i : i + 1, :], (PANEL, size)),
        )
        for i in range(PANEL)
    ]
    scale = [None] * PANEL
    low = {}
    for k in range(PANEL):
        scale[k] = 1.0 / s[k][k]
        for i in range(k + 1, PANEL):
            low[i, k] = s[k][i] * scale[k]
            for j in range(i, PANEL):
                s[i][j] = s[i][j] - low[i, k] * s[k][j]
            rows[i] = rows[i] - low[i, k] * rows[k]
    for k in range(PANEL):
        rows[k] = rows[k] * scale[k]
    for k in range(PANEL - 1, 0, -1):
        for i in range(k):
            rows[i] = rows[i] - low[k, i] * rows[k]
    solved = rows[0]
    for i in range(1, PANEL):
        solved = jnp.where(subs == i, rows[i], solved)
    fresh = [None] * count
    fresh[p] = solved
    for step in range(1, count):
        g = (p + step) % count
        col = [spread(a[g], i) for i in range(PANEL)]
        terms = [col[i] * rows[i] for i in range(PANEL)]
        while len(terms) > 1:
            terms = [terms[i] + terms[i + 1] for i in range(0, len(terms), 2)]
        fresh[g] = jnp.where(inside, 0.0, a[g]) - terms[0]
    return fresh


INNER = ((1,), (0,))
OUTER = ((1,), (1,))


def invert(s_ref, tile_ref):
    size = s_ref.shape[0]
    blocks = size // TILE

    @pl.loop(0, blocks)
    def _(k):
        at = pl.ds(pl.multiple_of(k * TILE, TILE), TILE)
        groups = [
            s_ref[pl.ds(pl.multiple_of(k * TILE, TILE) + PANEL * g, PANEL), at]
            for g in range(TILE // PANEL)
        ]
        for p in range(TILE // PANEL):
            groups = panel_step(groups, p)
        for g in range(TILE // PANEL):
            tile_ref[PANEL * g : PANEL * (g + 1), :] = groups[g]
        inverse = tile_ref[...]
        row = dot3(inverse, s_ref[at, :])
        s_ref[at, :] = row
        s_ref[at, at] = inverse
        row_parts = split(s_ref[at, :])
        for r in range(blocks):

            @pl.when(r != k)
            def _():
                rat = slice(r * TILE, (r + 1) * TILE)
                column = s_ref[rat, at]
                s_ref[rat, at] = jnp.zeros((TILE, TILE), F32)
                s_ref[rat, :] = s_ref[rat, :] - dot_parts(split(column), row_parts, INNER)


def kernel(
    tm_size, d_ref, u_ref, f_ref, dout_ref, uout_ref, fout_ref,
    s_ref, tile_ref, z_ref, full_ref, onward_ref, cur, scaled_ref, fresh_ref, ztiles, bufs, zbufs,
    send_sem, recv_sem, zsend_sem, zrecv_sem,
):
    half, size = d_ref.shape[1], d_ref.shape[2]
    column = lax.axis_index("col")
    place = lax.axis_index("tm")
    above, below = lax.rem(place + 1, tm_size), lax.rem(place + tm_size - 1, tm_size)
    over, under = lax.rem(place + 2, tm_size), lax.rem(place + tm_size - 2, tm_size)
    partner = 1 - column
    odd = lax.rem(place, 2) == 1
    even = lax.rem(place, 2) == 0
    has_left = place > 0
    has_right = place < tm_size - 1
    odd_right = jnp.logical_and(odd, has_right)
    even_left = jnp.logical_and(even, has_left)
    even_right = jnp.logical_and(even, place < tm_size - 2)
    own_at = pl.ds(pl.multiple_of(column * half, half), half)
    other_at = pl.ds(pl.multiple_of(partner * half, half), half)
    tile = half // 2

    barrier = pltpu.get_barrier_semaphore()

    def greet(where):
        pl.semaphore_signal(barrier, inc=1, device_id=where, device_id_type=pl.DeviceIdType.MESH)

    greet((place, partner))
    pl.when(has_left)(lambda: greet((below, column)))
    pl.when(has_right)(lambda: greet((above, column)))
    pl.when(even_left)(lambda: greet((under, column)))
    pl.when(even_right)(lambda: greet((over, column)))
    peers = [x.astype(jnp.int32) for x in (has_left, has_right, even_left, even_right)]
    pl.semaphore_wait(barrier, 1 + peers[0] + peers[1] + peers[2] + peers[3])

    targets = {"above": (above, column), "below": (below, column), "partner": (place, partner), "over": (over, column)}

    def copy(slot, source, target, landing=None):
        return pltpu.make_async_remote_copy(
            src_ref=source, dst_ref=bufs.at[slot] if landing is None else landing,
            send_sem=send_sem.at[slot], recv_sem=recv_sem.at[slot],
            device_id=targets[target], device_id_type=pl.DeviceIdType.MESH,
        )

    def copy_tiles(slot, source, target):
        return [
            pltpu.make_async_remote_copy(
                src_ref=source.at[i], dst_ref=zbufs.at[slot, i],
                send_sem=zsend_sem.at[ZTILES * slot + i], recv_sem=zrecv_sem.at[ZTILES * slot + i],
                device_id=targets[target], device_id_type=pl.DeviceIdType.MESH,
            )
            for i in range(ZTILES)
        ]

    def assemble(into, own, other):
        into[own_at, :] = own[...]
        into[other_at, :] = other[...]

    def tile_places(c):
        def at(row):
            return pl.ds(pl.multiple_of(row, tile), tile)

        first, far = c * half, (1 - c) * half
        near = [at(first), at(first + tile)]
        return [
            (near[0], near[0]), (near[0], near[1]), (near[1], near[1]),
            (near[0], at(far + c * tile)), (near[1], at(far + (1 - c) * tile)),
        ]

    def pack(z, into):
        for i, (row, col) in enumerate(tile_places(column)):
            into[i] = z[row, col]

    def unpack(slot, c):
        for i, (row, col) in enumerate(tile_places(c)):
            value = zbufs[slot, i]
            z_ref[row, col] = value
            if i not in (0, 2):
                z_ref[col, row] = value.T

    def receive(slot, other_slot, arriving, shared, onward=None, condition=None):
        for i in range(ZTILES):
            arriving[i].wait_recv()
            shared[i].start()
            if onward is not None:
                pl.when(condition)(onward[i].start)
        unpack(slot, column)
        for i in range(ZTILES):
            shared[i].wait_recv()
        unpack(other_slot, partner)

    def left(u, uother, f, d, s, dto, sto, keep=None):
        z = split(z_ref[...])
        own, other = split(u[...]), split(uother[...])
        for n, (values, base, out) in enumerate(((own, d, dto), (split(f[...]), s, sto))):
            scaled = dot_parts(values, z, INNER)
            if keep is not None:
                keep[n] = scaled
            scaled = split(scaled)
            out[:, own_at] = base[:, own_at] - dot_parts(scaled, own, OUTER)
            out[:, other_at] = base[:, other_at] - dot_parts(scaled, other, OUTER)

    def right_block(dto):
        z = split(z_ref[...])
        onward = split(full_ref[...])
        turned = dot_parts(split(full_ref[:, own_at]), z, ((0,), (0,)))
        dto[...] = dto[...] - dot_parts(split(turned), onward, INNER)

    def right(u, f, dto, uto, sto):
        z = split(z_ref[...])
        onward = split(full_ref[...])
        turned = dot_parts(split(full_ref[:, own_at]), z, ((0,), (0,)))
        dto[...] = dto[...] - dot_parts(split(turned), onward, INNER)
        solved = dot_parts(split(f[...]), z, INNER)
        sto[...] = sto[...] - dot_parts(split(solved), onward, INNER)
        scaled = dot_parts(split(u[...]), z, INNER)
        uto[...] = -dot_parts(split(scaled), onward, INNER)

    c_do = copy(DO, d_ref.at[1], "partner")
    c_uo = copy(UO, u_ref.at[1], "partner")
    c_eo = copy(EO, u_ref.at[0], "partner")
    c_e = copy(EB, u_ref.at[0], "below")
    c_ex = copy(EX, bufs.at[EB], "partner")
    c_ul = copy(UL, u_ref.at[1], "above")
    c_fl = copy(FL, f_ref.at[1], "above")
    c_fb = copy(FB, cur.at[2], "below")
    c_do1 = copy(DO1, cur.at[0], "partner")
    c_uo1 = copy(UO1, cur.at[1], "partner")
    c_uao = copy(UAO, fresh_ref.at[0], "partner")
    c_ul1 = copy(UL1, fresh_ref.at[0], "over")
    c_fl1 = copy(FL1, fresh_ref.at[1], "over")
    c_ru = copy(RU, fresh_ref.at[0], "above", uout_ref.at[0])
    c_rf = copy(RF, fresh_ref.at[1], "above", fout_ref.at[0])
    c_zl = copy_tiles(ZL, ztiles.at[0], "above")
    c_zlo = copy_tiles(ZLO, zbufs.at[ZL], "partner")
    c_za = copy_tiles(ZA, ztiles.at[1], "below")
    c_zao = copy_tiles(ZAO, zbufs.at[ZA], "partner")
    c_zl1 = copy_tiles(ZL1, zbufs.at[ZA], "over")
    c_zl1o = copy_tiles(ZL1O, zbufs.at[ZL1], "partner")

    c_do.start()
    pl.when(odd)(c_e.start)

    @pl.when(odd_right)
    def _():
        c_ul.start()
        c_fl.start()

    c_uo.start()
    c_eo.start()
    c_do.wait_recv()
    assemble(s_ref, d_ref.at[1], bufs.at[DO])
    invert(s_ref, tile_ref)
    pack(s_ref, ztiles.at[0])

    @pl.when(has_right)
    def _():
        for i in c_zl:
            i.start()

    c_uo.wait_recv()
    z_ref[...] = s_ref[...]
    left(
        u_ref.at[1], bufs.at[UO], f_ref.at[1], d_ref.at[0], f_ref.at[0], cur.at[0], cur.at[2], scaled_ref
    )
    c_eo.wait_recv()
    assemble(full_ref, u_ref.at[0], bufs.at[EO])
    dout_ref[1] = d_ref[1]
    uout_ref[1] = u_ref[1]
    fout_ref[1] = f_ref[1]

    @pl.when(odd)
    def _():
        c_fb.start()
        receive(ZL, ZLO, c_zl, c_zlo)
        right_block(cur.at[0])
        c_do1.start()
        dout_ref[0] = cur[0]
        c_do1.wait_recv()
        assemble(s_ref, cur.at[0], bufs.at[DO1])
        invert(s_ref, tile_ref)
        pack(s_ref, ztiles.at[1])
        for i in c_za:
            i.start()
        c_ru.wait_recv()
        c_rf.wait_recv()

    @pl.when(even)
    def _():
        c_e.wait_recv()
        c_ex.start()
        c_ex.wait_recv()
        assemble(onward_ref, bufs.at[EB], bufs.at[EX])
        fresh_ref[0] = -dot3(scaled_ref[0], onward_ref[...])
        c_ru.start()
        c_uao.start()
        pl.when(even_right)(c_ul1.start)
        cur[1] = u_ref[0]

        @pl.when(has_left)
        def _():
            c_ul.wait_recv()
            c_fl.wait_recv()
            receive(ZL, ZLO, c_zl, c_zlo)
            right(bufs.at[UL], bufs.at[FL], cur.at[0], cur.at[1], cur.at[2])

        c_uo1.start()
        c_fb.wait_recv()
        fresh_ref[1] = bufs[FB] - dot3(scaled_ref[1], onward_ref[...])
        c_rf.start()
        pl.when(even_right)(c_fl1.start)
        c_uo1.wait_recv()
        assemble(full_ref, cur.at[1], bufs.at[UO1])
        uout_ref[0] = cur[1]
        c_uao.wait_recv()
        receive(ZA, ZAO, c_za, c_zao, c_zl1, even_right)
        left(
            fresh_ref.at[0], bufs.at[UAO], fresh_ref.at[1], cur.at[0], cur.at[2], dout_ref.at[0], fout_ref.at[0]
        )

    @pl.when(even_left)
    def _():
        c_ul1.wait_recv()
        c_fl1.wait_recv()
        receive(ZL1, ZL1O, c_zl1, c_zl1o)
        right(bufs.at[UL1], bufs.at[FL1], dout_ref.at[0], uout_ref.at[0], fout_ref.at[0])

    def drained(condition, copies):
        @pl.when(condition)
        def _():
            for i in copies:
                i.wait_send()

    for i in (c_do, c_uo, c_eo):
        i.wait_send()
    drained(has_right, c_zl)
    drained(has_left, c_zlo)
    drained(odd_right, [c_ul, c_fl])
    drained(odd, [c_e, c_fb, c_do1] + c_za)
    drained(even, [c_ex, c_ru, c_rf, c_uao, c_uo1] + c_zao)
    drained(even_right, [c_ul1, c_fl1] + c_zl1)
    drained(even_left, c_zl1o)


SLOTS = 15
DO, UO, EO, EB, EX, UL, FL, FB, DO1, UO1, UAO, UL1, FL1, RU, RF = range(SLOTS)
ZSLOTS = 6
ZL, ZLO, ZA, ZAO, ZL1, ZL1O = range(ZSLOTS)
ZTILES = 5


def body(tm_size, diagonal_blocks, upper_blocks, right_sides):
    shape = diagonal_blocks.shape
    half, size = shape[1], shape[2]
    tile = half // 2
    whole = pl.BlockSpec(memory_space=pltpu.VMEM)
    return pl.pallas_call(
        functools.partial(kernel, tm_size),
        out_shape=[jax.ShapeDtypeStruct(shape, F32)] * 3,
        in_specs=[whole] * 3,
        out_specs=[whole] * 3,
        scratch_shapes=[
            pltpu.VMEM((size, size), F32),
            pltpu.VMEM((TILE, TILE), F32),
            pltpu.VMEM((size, size), F32),
            pltpu.VMEM((size, size), F32),
            pltpu.VMEM((size, size), F32),
            pltpu.VMEM((3, half, size), F32),
            pltpu.VMEM((2, half, size), F32),
            pltpu.VMEM((2, half, size), F32),
            pltpu.VMEM((2, ZTILES, tile, tile), F32),
            pltpu.VMEM((RU, half, size), F32),
            pltpu.VMEM((ZSLOTS, ZTILES, tile, tile), F32),
            pltpu.SemaphoreType.DMA((SLOTS,)),
            pltpu.SemaphoreType.DMA((SLOTS,)),
            pltpu.SemaphoreType.DMA((ZSLOTS * ZTILES,)),
            pltpu.SemaphoreType.DMA((ZSLOTS * ZTILES,)),
        ],
        compiler_params=pltpu.CompilerParams(
            vmem_limit_bytes=50 * 2**20, collective_id=0, has_side_effects=True
        ),
        name="reduce_levels",
    )(diagonal_blocks, upper_blocks, right_sides)


def solution(mesh):
    placed = (P("tm", "col", None),) * 3
    return jax.shard_map(
        functools.partial(body, mesh.shape["tm"]),
        mesh=mesh,
        in_specs=placed,
        out_specs=placed,
        check_vma=False,
    )
```

```python
import functools

import jax
import jax.numpy as jnp
from jax import lax
from jax.experimental import pallas as pl
from jax.experimental.pallas import tpu as pltpu
from jax.sharding import PartitionSpec as P

LEVELS = 2
TILE = 128
PANEL = 8
F32 = jnp.float32
BF16 = jnp.bfloat16


def split(values):
    high = values.astype(BF16)
    return high, (values - high.astype(F32)).astype(BF16)


def dot_parts(left, right, dims):
    def one(a, b):
        return lax.dot_general(a, b, (dims, ((), ())), preferred_element_type=F32)

    return one(left[0], right[0]) + (one(left[0], right[1]) + one(left[1], right[0]))


def dot3(left, right, dims=((1,), (0,))):
    return dot_parts(split(left), split(right), dims)


def panel_step(a, p):
    size = a[0].shape[1]
    count = size // PANEL
    base = PANEL * p
    lanes = lax.broadcasted_iota(jnp.int32, (PANEL, size), 1)
    subs = lax.broadcasted_iota(jnp.int32, (PANEL, size), 0)
    inside = jnp.logical_and(lanes >= base, lanes < base + PANEL)

    def spread(values, i):
        return jnp.broadcast_to(values[:, base + i : base + i + 1], (PANEL, size))

    head = [spread(a[p], i) for i in range(PANEL)]
    s = [
        [jnp.broadcast_to(head[j][i : i + 1, :], (PANEL, size)) if j >= i else None for j in range(PANEL)]
        for i in range(PANEL)
    ]
    rows = [
        jnp.where(
            inside,
            jnp.where(lanes == base + i, 1.0, 0.0),
            jnp.broadcast_to(a[p][i : i + 1, :], (PANEL, size)),
        )
        for i in range(PANEL)
    ]
    scale = [None] * PANEL
    low = {}
    for k in range(PANEL):
        scale[k] = 1.0 / s[k][k]
        for i in range(k + 1, PANEL):
            low[i, k] = s[k][i] * scale[k]
            for j in range(i, PANEL):
                s[i][j] = s[i][j] - low[i, k] * s[k][j]
            rows[i] = rows[i] - low[i, k] * rows[k]
    for k in range(PANEL):
        rows[k] = rows[k] * scale[k]
    for k in range(PANEL - 1, 0, -1):
        for i in range(k):
            rows[i] = rows[i] - low[k, i] * rows[k]
    solved = rows[0]
    for i in range(1, PANEL):
        solved = jnp.where(subs == i, rows[i], solved)
    fresh = [None] * count
    fresh[p] = solved
    for step in range(1, count):
        g = (p + step) % count
        col = [spread(a[g], i) for i in range(PANEL)]
        terms = [col[i] * rows[i] for i in range(PANEL)]
        while len(terms) > 1:
            terms = [terms[i] + terms[i + 1] for i in range(0, len(terms), 2)]
        fresh[g] = jnp.where(inside, 0.0, a[g]) - terms[0]
    return fresh


INNER = ((1,), (0,))
OUTER = ((1,), (1,))


def invert(s_ref, tile_ref, fac_ref, col_ref, ready, send):
    blocks = s_ref.shape[0] // TILE
    steps = TILE // PANEL

    def span(index):
        return pl.ds(pl.multiple_of(index * TILE, TILE), TILE)

    def fixed(index):
        return slice(index * TILE, (index + 1) * TILE)

    def take_column(k):
        for o in range(blocks - 1):
            rat = span(lax.rem(k + o + 1, blocks))
            col_ref[o] = s_ref[rat, span(k)]
            s_ref[rat, span(k)] = jnp.zeros((TILE, TILE), F32)

    def row_job(k, c):
        inverse = tile_ref[...]
        value = jnp.where(k == c, inverse, dot3(inverse, s_ref[span(k), fixed(c)]))
        fac_ref[k, c] = value
        s_ref[span(k), fixed(c)] = value

    def update_job(k, o, c):
        rat = span(lax.rem(k + o + 1, blocks))
        s_ref[rat, fixed(c)] = s_ref[rat, fixed(c)] - dot3(col_ref[o], fac_ref[k, c])

    def invert_tile(k, jobs):
        groups = [
            s_ref[pl.ds(pl.multiple_of(k * TILE, TILE) + PANEL * g, PANEL), span(k)] for g in range(steps)
        ]
        for p in range(steps):
            groups = panel_step(groups, p)
            for job in jobs[p * len(jobs) // steps : (p + 1) * len(jobs) // steps]:
                job()
        for g in range(steps):
            tile_ref[PANEL * g : PANEL * (g + 1), :] = groups[g]

    invert_tile(0, [])
    ready()

    @pl.loop(1, blocks)
    def _(k):
        last = k - 1
        take_column(last)
        row = dot3(tile_ref[...], s_ref[span(last), span(k)])
        s_ref[span(k), span(k)] = s_ref[span(k), span(k)] - dot3(col_ref[0], row)
        jobs = [functools.partial(row_job, last, c) for c in range(blocks)]
        jobs.append(lambda: send(last))
        for o in range(blocks - 1):
            jobs += [functools.partial(update_job, last, o, c) for c in range(blocks)]
        invert_tile(k, jobs)

    end = blocks - 1
    fac_ref[end, end] = tile_ref[...]
    send(end)
    take_column(end)
    s_ref[fixed(end), fixed(end)] = tile_ref[...]
    for c in range(end):
        row_job(end, c)
    for o in range(blocks - 1):
        for c in range(blocks):
            update_job(end, o, c)


def kernel(
    tm_size, d_ref, u_ref, f_ref, dout_ref, uout_ref, fout_ref,
    s_ref, tile_ref, fac_ref, col_ref, z_ref, full_ref, onward_ref, cur, scaled_ref, fresh_ref, ztiles, bufs, zbufs, fbufs,
    send_sem, recv_sem, zsend_sem, zrecv_sem, fsend_sem, frecv_sem,
):
    half, size = d_ref.shape[1], d_ref.shape[2]
    column = lax.axis_index("col")
    place = lax.axis_index("tm")
    above, below = lax.rem(place + 1, tm_size), lax.rem(place + tm_size - 1, tm_size)
    over, under = lax.rem(place + 2, tm_size), lax.rem(place + tm_size - 2, tm_size)
    partner = 1 - column
    odd = lax.rem(place, 2) == 1
    even = lax.rem(place, 2) == 0
    has_left = place > 0
    has_right = place < tm_size - 1
    odd_right = jnp.logical_and(odd, has_right)
    even_left = jnp.logical_and(even, has_left)
    even_right = jnp.logical_and(even, place < tm_size - 2)
    own_at = pl.ds(pl.multiple_of(column * half, half), half)
    other_at = pl.ds(pl.multiple_of(partner * half, half), half)
    tile = half // 2

    barrier = pltpu.get_barrier_semaphore()

    def greet(where):
        pl.semaphore_signal(barrier, inc=1, device_id=where, device_id_type=pl.DeviceIdType.MESH)

    greet((place, partner))
    pl.when(has_left)(lambda: greet((below, column)))
    pl.when(has_right)(lambda: greet((above, column)))
    pl.when(even_left)(lambda: greet((under, column)))
    pl.when(even_right)(lambda: greet((over, column)))
    peers = [x.astype(jnp.int32) for x in (has_left, has_right, even_left, even_right)]
    pl.semaphore_wait(barrier, 1 + peers[0] + peers[1] + peers[2] + peers[3])

    targets = {"above": (above, column), "below": (below, column), "partner": (place, partner), "over": (over, column)}

    def copy(slot, source, target, landing=None):
        return pltpu.make_async_remote_copy(
            src_ref=source, dst_ref=bufs.at[slot] if landing is None else landing,
            send_sem=send_sem.at[slot], recv_sem=recv_sem.at[slot],
            device_id=targets[target], device_id_type=pl.DeviceIdType.MESH,
        )

    def copy_tiles(slot, source, target):
        return [
            pltpu.make_async_remote_copy(
                src_ref=source.at[i], dst_ref=zbufs.at[slot, i],
                send_sem=zsend_sem.at[ZTILES * slot + i], recv_sem=zrecv_sem.at[ZTILES * slot + i],
                device_id=targets[target], device_id_type=pl.DeviceIdType.MESH,
            )
            for i in range(ZTILES)
        ]

    def assemble(into, own, other):
        into[own_at, :] = own[...]
        into[other_at, :] = other[...]

    def tile_places(c):
        def at(row):
            return pl.ds(pl.multiple_of(row, tile), tile)

        first, far = c * half, (1 - c) * half
        near = [at(first), at(first + tile)]
        return [
            (near[0], near[0]), (near[0], near[1]), (near[1], near[1]),
            (near[0], at(far + c * tile)), (near[1], at(far + (1 - c) * tile)),
        ]

    def pack(into):
        places = [(0, 0), (0, tile), (tile, tile), (0, half + column * tile), (tile, half + partner * tile)]
        for i, (row, col) in enumerate(places):
            into[i] = s_ref[row : row + tile, pl.ds(pl.multiple_of(col, tile), tile)]

    def fill_own(source):
        s_ref[:half, :half] = source[:, own_at]
        s_ref[:half, half:] = source[:, other_at]

    def fill_other(source):
        s_ref[half:, :half] = source[:, own_at]
        s_ref[half:, half:] = source[:, other_at]

    def store_inverse():
        z_ref[own_at, own_at] = s_ref[:half, :half]
        z_ref[own_at, other_at] = s_ref[:half, half:]
        z_ref[other_at, own_at] = s_ref[half:, :half]
        z_ref[other_at, other_at] = s_ref[half:, half:]

    blocks = size // TILE

    def copy_factor(k, c):
        sem = k * blocks + c
        return pltpu.make_async_remote_copy(
            src_ref=fac_ref.at[k, c], dst_ref=fbufs.at[k, c],
            send_sem=fsend_sem.at[sem], recv_sem=frecv_sem.at[sem],
            device_id=targets["above"], device_id_type=pl.DeviceIdType.MESH,
        )

    def send_factor(k):
        for c in range(blocks):
            pl.when(jnp.logical_and(even, c >= k))(copy_factor(k, c).start)

    def unpack(slot, c):
        for i, (row, col) in enumerate(tile_places(c)):
            value = zbufs[slot, i]
            z_ref[row, col] = value
            if i not in (0, 2):
                z_ref[col, row] = value.T

    def receive(slot, other_slot, arriving, shared, onward=None, condition=None):
        for i in range(ZTILES):
            arriving[i].wait_recv()
            shared[i].start()
            if onward is not None:
                pl.when(condition)(onward[i].start)
        unpack(slot, column)
        for i in range(ZTILES):
            shared[i].wait_recv()
        unpack(other_slot, partner)

    def left(u, uother, f, d, s, dto, sto, keep=None):
        z = split(z_ref[...])
        own, other = split(u[...]), split(uother[...])
        for n, (values, base, out) in enumerate(((own, d, dto), (split(f[...]), s, sto))):
            scaled = dot_parts(values, z, INNER)
            if keep is not None:
                keep[n] = scaled
            scaled = split(scaled)
            out[:, own_at] = base[:, own_at] - dot_parts(scaled, own, OUTER)
            out[:, other_at] = base[:, other_at] - dot_parts(scaled, other, OUTER)

    def right_block(dto):
        for m in range(blocks):
            at = slice(m * TILE, (m + 1) * TILE)
            for c in range(m, blocks):
                copy_factor(m, c).wait_recv()
            onward_ref[at] = dot3(fbufs[m, m], full_ref[at])
            for c in range(m + 1, blocks):
                rat = slice(c * TILE, (c + 1) * TILE)
                full_ref[rat] = full_ref[rat] - dot3(fbufs[m, c], full_ref[at], ((0,), (0,)))
        dto[...] = dto[...] - dot3(full_ref[:, own_at], onward_ref[...], ((0,), (0,)))

    def right(u, f, dto, uto, sto):
        z = split(z_ref[...])
        onward = split(full_ref[...])
        turned = dot_parts(split(full_ref[:, own_at]), z, ((0,), (0,)))
        dto[...] = dto[...] - dot_parts(split(turned), onward, INNER)
        solved = dot_parts(split(f[...]), z, INNER)
        sto[...] = sto[...] - dot_parts(split(solved), onward, INNER)
        scaled = dot_parts(split(u[...]), z, INNER)
        uto[...] = -dot_parts(split(scaled), onward, INNER)

    c_do = copy(DO, d_ref.at[1], "partner")
    c_uo = copy(UO, u_ref.at[1], "partner")
    c_eo = copy(EO, u_ref.at[0], "partner")
    c_e = copy(EB, u_ref.at[0], "below")
    c_ex = copy(EX, bufs.at[EB], "partner")
    c_ul = copy(UL, u_ref.at[1], "above")
    c_fl = copy(FL, f_ref.at[1], "above")
    c_fb = copy(FB, cur.at[2], "below")
    c_do1 = copy(DO1, cur.at[0], "partner")
    c_uo1 = copy(UO1, cur.at[1], "partner")
    c_uao = copy(UAO, fresh_ref.at[0], "partner")
    c_ul1 = copy(UL1, fresh_ref.at[0], "over")
    c_fl1 = copy(FL1, fresh_ref.at[1], "over")
    c_ru = copy(RU, fresh_ref.at[0], "above", uout_ref.at[0])
    c_rf = copy(RF, fresh_ref.at[1], "above", fout_ref.at[0])
    c_zl = copy_tiles(ZL, ztiles.at[0], "above")
    c_zlo = copy_tiles(ZLO, zbufs.at[ZL], "partner")
    c_za = copy_tiles(ZA, ztiles.at[1], "below")
    c_zao = copy_tiles(ZAO, zbufs.at[ZA], "partner")
    c_zl1 = copy_tiles(ZL1, zbufs.at[ZA], "over")
    c_zl1o = copy_tiles(ZL1O, zbufs.at[ZL1], "partner")

    c_do.start()
    pl.when(odd)(c_e.start)

    @pl.when(odd_right)
    def _():
        c_ul.start()
        c_fl.start()

    c_uo.start()
    c_eo.start()
    fill_own(d_ref.at[1])

    def ready():
        c_do.wait_recv()
        fill_other(bufs.at[DO])

    invert(s_ref, tile_ref, fac_ref, col_ref, ready, send_factor)

    @pl.when(odd_right)
    def _():
        pack(ztiles.at[0])
        for i in c_zl:
            i.start()

    store_inverse()
    c_uo.wait_recv()
    left(
        u_ref.at[1], bufs.at[UO], f_ref.at[1], d_ref.at[0], f_ref.at[0], cur.at[0], cur.at[2], scaled_ref
    )
    c_eo.wait_recv()
    dout_ref[1] = d_ref[1]
    uout_ref[1] = u_ref[1]
    fout_ref[1] = f_ref[1]

    @pl.when(odd)
    def _():
        c_fb.start()
        full_ref[:half] = u_ref[0]
        full_ref[half:] = bufs[EO]
        right_block(cur.at[0])
        c_do1.start()
        fill_own(cur.at[0])

        def ready():
            c_do1.wait_recv()
            fill_other(bufs.at[DO1])
            dout_ref[0] = cur[0]

        invert(s_ref, tile_ref, fac_ref, col_ref, ready, lambda k: None)
        pack(ztiles.at[1])
        for i in c_za:
            i.start()
        c_ru.wait_recv()
        c_rf.wait_recv()

    @pl.when(even)
    def _():
        c_e.wait_recv()
        c_ex.start()
        c_ex.wait_recv()
        assemble(onward_ref, bufs.at[EB], bufs.at[EX])
        fresh_ref[0] = -dot3(scaled_ref[0], onward_ref[...])
        c_ru.start()
        c_uao.start()
        pl.when(even_right)(c_ul1.start)
        cur[1] = u_ref[0]

        @pl.when(has_left)
        def _():
            c_ul.wait_recv()
            c_fl.wait_recv()
            receive(ZL, ZLO, c_zl, c_zlo)
            assemble(full_ref, u_ref.at[0], bufs.at[EO])
            right(bufs.at[UL], bufs.at[FL], cur.at[0], cur.at[1], cur.at[2])

        c_uo1.start()
        c_fb.wait_recv()
        fresh_ref[1] = bufs[FB] - dot3(scaled_ref[1], onward_ref[...])
        c_rf.start()
        pl.when(even_right)(c_fl1.start)
        c_uo1.wait_recv()
        assemble(full_ref, cur.at[1], bufs.at[UO1])
        uout_ref[0] = cur[1]
        c_uao.wait_recv()
        receive(ZA, ZAO, c_za, c_zao, c_zl1, even_right)
        left(
            fresh_ref.at[0], bufs.at[UAO], fresh_ref.at[1], cur.at[0], cur.at[2], dout_ref.at[0], fout_ref.at[0]
        )

    @pl.when(even_left)
    def _():
        c_ul1.wait_recv()
        c_fl1.wait_recv()
        receive(ZL1, ZL1O, c_zl1, c_zl1o)
        right(bufs.at[UL1], bufs.at[FL1], dout_ref.at[0], uout_ref.at[0], fout_ref.at[0])

    def drained(condition, copies):
        @pl.when(condition)
        def _():
            for i in copies:
                i.wait_send()

    for i in (c_do, c_uo, c_eo):
        i.wait_send()
    drained(odd_right, [c_ul, c_fl] + c_zl)
    drained(even_left, c_zlo)
    drained(even, [copy_factor(k, c) for k in range(blocks) for c in range(k, blocks)])
    drained(odd, [c_e, c_fb, c_do1] + c_za)
    drained(even, [c_ex, c_ru, c_rf, c_uao, c_uo1] + c_zao)
    drained(even_right, [c_ul1, c_fl1] + c_zl1)
    drained(even_left, c_zl1o)


SLOTS = 15
DO, UO, EO, EB, EX, UL, FL, FB, DO1, UO1, UAO, UL1, FL1, RU, RF = range(SLOTS)
ZSLOTS = 6
ZL, ZLO, ZA, ZAO, ZL1, ZL1O = range(ZSLOTS)
ZTILES = 5


def body(tm_size, diagonal_blocks, upper_blocks, right_sides):
    shape = diagonal_blocks.shape
    half, size = shape[1], shape[2]
    tile, blocks = half // 2, size // TILE
    whole = pl.BlockSpec(memory_space=pltpu.VMEM)
    return pl.pallas_call(
        functools.partial(kernel, tm_size),
        out_shape=[jax.ShapeDtypeStruct(shape, F32)] * 3,
        in_specs=[whole] * 3,
        out_specs=[whole] * 3,
        scratch_shapes=[
            pltpu.VMEM((size, size), F32),
            pltpu.VMEM((TILE, TILE), F32),
            pltpu.VMEM((blocks, blocks, TILE, TILE), F32),
            pltpu.VMEM((blocks - 1, TILE, TILE), F32),
            pltpu.VMEM((size, size), F32),
            pltpu.VMEM((size, size), F32),
            pltpu.VMEM((size, size), F32),
            pltpu.VMEM((3, half, size), F32),
            pltpu.VMEM((2, half, size), F32),
            pltpu.VMEM((2, half, size), F32),
            pltpu.VMEM((2, ZTILES, tile, tile), F32),
            pltpu.VMEM((RU, half, size), F32),
            pltpu.VMEM((ZSLOTS, ZTILES, tile, tile), F32),
            pltpu.VMEM((blocks, blocks, TILE, TILE), F32),
            pltpu.SemaphoreType.DMA((SLOTS,)),
            pltpu.SemaphoreType.DMA((SLOTS,)),
            pltpu.SemaphoreType.DMA((ZSLOTS * ZTILES,)),
            pltpu.SemaphoreType.DMA((ZSLOTS * ZTILES,)),
            pltpu.SemaphoreType.DMA((blocks * blocks,)),
            pltpu.SemaphoreType.DMA((blocks * blocks,)),
        ],
        compiler_params=pltpu.CompilerParams(
            vmem_limit_bytes=50 * 2**20, collective_id=0, has_side_effects=True
        ),
        name="reduce_levels",
    )(diagonal_blocks, upper_blocks, right_sides)


def solution(mesh):
    placed = (P("tm", "col", None),) * 3
    return jax.shard_map(
        functools.partial(body, mesh.shape["tm"]),
        mesh=mesh,
        in_specs=placed,
        out_specs=placed,
        check_vma=False,
    )
```

```python
import functools

import jax
import jax.numpy as jnp
from jax import lax
from jax.experimental import pallas as pl
from jax.experimental.pallas import tpu as pltpu
from jax.sharding import PartitionSpec as P

LEVELS = 2
TILE = 128
PANEL = 8
F32 = jnp.float32
BF16 = jnp.bfloat16


def split(values):
    high = values.astype(BF16)
    return high, (values - high.astype(F32)).astype(BF16)


def dot_parts(left, right, dims):
    def one(a, b):
        return lax.dot_general(a, b, (dims, ((), ())), preferred_element_type=F32)

    return one(left[0], right[0]) + (one(left[0], right[1]) + one(left[1], right[0]))


def dot3(left, right, dims=((1,), (0,))):
    return dot_parts(split(left), split(right), dims)


def panel_step(a, p):
    size = a[0].shape[1]
    count = size // PANEL
    base = PANEL * p
    lanes = lax.broadcasted_iota(jnp.int32, (PANEL, size), 1)
    subs = lax.broadcasted_iota(jnp.int32, (PANEL, size), 0)
    inside = jnp.logical_and(lanes >= base, lanes < base + PANEL)

    def spread(values, i):
        return jnp.broadcast_to(values[:, base + i : base + i + 1], (PANEL, size))

    head = [spread(a[p], i) for i in range(PANEL)]
    s = [
        [jnp.broadcast_to(head[j][i : i + 1, :], (PANEL, size)) if j >= i else None for j in range(PANEL)]
        for i in range(PANEL)
    ]
    rows = [
        jnp.where(
            inside,
            jnp.where(lanes == base + i, 1.0, 0.0),
            jnp.broadcast_to(a[p][i : i + 1, :], (PANEL, size)),
        )
        for i in range(PANEL)
    ]
    scale = [None] * PANEL
    low = {}
    for k in range(PANEL):
        scale[k] = 1.0 / s[k][k]
        for i in range(k + 1, PANEL):
            low[i, k] = s[k][i] * scale[k]
            for j in range(i, PANEL):
                s[i][j] = s[i][j] - low[i, k] * s[k][j]
            rows[i] = rows[i] - low[i, k] * rows[k]
    for k in range(PANEL):
        rows[k] = rows[k] * scale[k]
    for k in range(PANEL - 1, 0, -1):
        for i in range(k):
            rows[i] = rows[i] - low[k, i] * rows[k]
    solved = rows[0]
    for i in range(1, PANEL):
        solved = jnp.where(subs == i, rows[i], solved)
    fresh = [None] * count
    fresh[p] = solved
    for step in range(1, count):
        g = (p + step) % count
        col = [spread(a[g], i) for i in range(PANEL)]
        terms = [col[i] * rows[i] for i in range(PANEL)]
        while len(terms) > 1:
            terms = [terms[i] + terms[i + 1] for i in range(0, len(terms), 2)]
        fresh[g] = jnp.where(inside, 0.0, a[g]) - terms[0]
    return fresh


INNER = ((1,), (0,))
OUTER = ((1,), (1,))


def invert(s_ref, tile_ref, fac_ref, col_ref, ready, send, after):
    blocks = s_ref.shape[0] // TILE
    steps = TILE // PANEL

    def span(index):
        return pl.ds(pl.multiple_of(index * TILE, TILE), TILE)

    def fixed(index):
        return slice(index * TILE, (index + 1) * TILE)

    def take_column(k):
        for o in range(blocks - 1):
            rat = span(lax.rem(k + o + 1, blocks))
            col_ref[o] = s_ref[rat, span(k)]
            s_ref[rat, span(k)] = jnp.zeros((TILE, TILE), F32)

    def row_job(k, c):
        inverse = tile_ref[...]
        value = jnp.where(k == c, inverse, dot3(inverse, s_ref[span(k), fixed(c)]))
        fac_ref[k, c] = value
        s_ref[span(k), fixed(c)] = value

    def update_job(k, o, c):
        rat = span(lax.rem(k + o + 1, blocks))
        s_ref[rat, fixed(c)] = s_ref[rat, fixed(c)] - dot3(col_ref[o], fac_ref[k, c])

    def invert_tile(k, jobs):
        groups = [
            s_ref[pl.ds(pl.multiple_of(k * TILE, TILE) + PANEL * g, PANEL), span(k)] for g in range(steps)
        ]
        for p in range(steps):
            groups = panel_step(groups, p)
            for job in jobs[p * len(jobs) // steps : (p + 1) * len(jobs) // steps]:
                job()
        for g in range(steps):
            tile_ref[PANEL * g : PANEL * (g + 1), :] = groups[g]

    invert_tile(0, [])
    ready()

    @pl.loop(1, blocks)
    def _(k):
        last = k - 1
        take_column(last)
        row = dot3(tile_ref[...], s_ref[span(last), span(k)])
        s_ref[span(k), span(k)] = s_ref[span(k), span(k)] - dot3(col_ref[0], row)
        jobs = [functools.partial(row_job, last, c) for c in range(blocks)]
        jobs.append(lambda: send(last))
        for o in range(blocks - 1):
            jobs += [functools.partial(update_job, last, o, c) for c in range(blocks)]
        invert_tile(k, jobs)
        after(k)

    end = blocks - 1
    fac_ref[end, end] = tile_ref[...]
    send(end)
    take_column(end)
    s_ref[fixed(end), fixed(end)] = tile_ref[...]
    for c in range(end):
        row_job(end, c)
    for o in range(blocks - 1):
        for c in range(blocks):
            update_job(end, o, c)


def kernel(
    tm_size, d_ref, u_ref, f_ref, dout_ref, uout_ref, fout_ref,
    s_ref, tile_ref, fac_ref, col_ref, z_ref, full_ref, onward_ref, ahead_ref, cur, scaled_ref, fresh_ref, ztiles, bufs, zbufs, fbufs,
    send_sem, recv_sem, zsend_sem, zrecv_sem, fsend_sem, frecv_sem,
):
    half, size = d_ref.shape[1], d_ref.shape[2]
    column = lax.axis_index("col")
    place = lax.axis_index("tm")
    above, below = lax.rem(place + 1, tm_size), lax.rem(place + tm_size - 1, tm_size)
    over, under = lax.rem(place + 2, tm_size), lax.rem(place + tm_size - 2, tm_size)
    partner = 1 - column
    odd = lax.rem(place, 2) == 1
    even = lax.rem(place, 2) == 0
    has_left = place > 0
    has_right = place < tm_size - 1
    has_under, has_over = place > 1, place < tm_size - 2
    odd_over = jnp.logical_and(odd, has_over)
    odd_under = jnp.logical_and(odd, has_under)
    even_left = jnp.logical_and(even, has_under)
    even_right = jnp.logical_and(even, has_over)
    own_at = pl.ds(pl.multiple_of(column * half, half), half)
    other_at = pl.ds(pl.multiple_of(partner * half, half), half)
    tile = half // 2

    barrier = pltpu.get_barrier_semaphore()

    def greet(where):
        pl.semaphore_signal(barrier, inc=1, device_id=where, device_id_type=pl.DeviceIdType.MESH)

    greet((place, partner))
    pl.when(has_left)(lambda: greet((below, column)))
    pl.when(has_right)(lambda: greet((above, column)))
    pl.when(has_under)(lambda: greet((under, column)))
    pl.when(has_over)(lambda: greet((over, column)))
    peers = [x.astype(jnp.int32) for x in (has_left, has_right, has_under, has_over)]
    pl.semaphore_wait(barrier, 1 + peers[0] + peers[1] + peers[2] + peers[3])

    targets = {"above": (above, column), "below": (below, column), "partner": (place, partner), "over": (over, column)}

    def copy(slot, source, target, landing=None):
        return pltpu.make_async_remote_copy(
            src_ref=source, dst_ref=bufs.at[slot] if landing is None else landing,
            send_sem=send_sem.at[slot], recv_sem=recv_sem.at[slot],
            device_id=targets[target], device_id_type=pl.DeviceIdType.MESH,
        )

    def copy_tiles(slot, source, target):
        return [
            pltpu.make_async_remote_copy(
                src_ref=source.at[i], dst_ref=zbufs.at[slot, i],
                send_sem=zsend_sem.at[ZTILES * slot + i], recv_sem=zrecv_sem.at[ZTILES * slot + i],
                device_id=targets[target], device_id_type=pl.DeviceIdType.MESH,
            )
            for i in range(ZTILES)
        ]

    def assemble(into, own, other):
        into[own_at, :] = own[...]
        into[other_at, :] = other[...]

    def tile_places(c):
        def at(row):
            return pl.ds(pl.multiple_of(row, tile), tile)

        first, far = c * half, (1 - c) * half
        near = [at(first), at(first + tile)]
        return [
            (near[0], near[0]), (near[0], near[1]), (near[1], near[1]),
            (near[0], at(far + c * tile)), (near[1], at(far + (1 - c) * tile)),
        ]

    def pack(into):
        places = [(0, 0), (0, tile), (tile, tile), (0, half + column * tile), (tile, half + partner * tile)]
        for i, (row, col) in enumerate(places):
            into[i] = s_ref[row : row + tile, pl.ds(pl.multiple_of(col, tile), tile)]

    def fill_own(source):
        s_ref[:half, :half] = source[:, own_at]
        s_ref[:half, half:] = source[:, other_at]

    def fill_other(source):
        s_ref[half:, :half] = source[:, own_at]
        s_ref[half:, half:] = source[:, other_at]

    def store_inverse():
        z_ref[own_at, own_at] = s_ref[:half, :half]
        z_ref[own_at, other_at] = s_ref[:half, half:]
        z_ref[other_at, own_at] = s_ref[half:, :half]
        z_ref[other_at, other_at] = s_ref[half:, half:]

    blocks = size // TILE

    def copy_factor(k, c):
        sem = k * blocks + c
        return pltpu.make_async_remote_copy(
            src_ref=fac_ref.at[k, c], dst_ref=fbufs.at[k, c],
            send_sem=fsend_sem.at[sem], recv_sem=frecv_sem.at[sem],
            device_id=targets["above"], device_id_type=pl.DeviceIdType.MESH,
        )

    def send_factor(k):
        for c in range(blocks):
            pl.when(jnp.logical_and(even, c >= k))(copy_factor(k, c).start)

    def unpack(slot, c):
        for i, (row, col) in enumerate(tile_places(c)):
            value = zbufs[slot, i]
            z_ref[row, col] = value
            if i not in (0, 2):
                z_ref[col, row] = value.T

    def receive(slot, other_slot, arriving, shared, onward=None, condition=None):
        for i in range(ZTILES):
            arriving[i].wait_recv()
            shared[i].start()
            if onward is not None:
                pl.when(condition)(onward[i].start)
        unpack(slot, column)
        for i in range(ZTILES):
            shared[i].wait_recv()
        unpack(other_slot, partner)

    def left(u, uother, f, d, s, dto, sto, keep=None):
        z = split(z_ref[...])
        own, other = split(u[...]), split(uother[...])
        for n, (values, base, out) in enumerate(((own, d, dto), (split(f[...]), s, sto))):
            scaled = dot_parts(values, z, INNER)
            if keep is not None:
                keep[n] = scaled
            scaled = split(scaled)
            out[:, own_at] = base[:, own_at] - dot_parts(scaled, own, OUTER)
            out[:, other_at] = base[:, other_at] - dot_parts(scaled, other, OUTER)

    def right_block(dto):
        for m in range(blocks):
            at = slice(m * TILE, (m + 1) * TILE)
            for c in range(m, blocks):
                copy_factor(m, c).wait_recv()
            onward_ref[at] = dot3(fbufs[m, m], full_ref[at])
            for c in range(m + 1, blocks):
                rat = slice(c * TILE, (c + 1) * TILE)
                full_ref[rat] = full_ref[rat] - dot3(fbufs[m, c], full_ref[at], ((0,), (0,)))
        dto[...] = dto[...] - dot3(full_ref[:, own_at], onward_ref[...], ((0,), (0,)))

    def ahead(into):
        into[...] = dot3(z_ref[...], full_ref[...])

    def right(product_ref, u, dto, uto):
        product = split(product_ref[...])
        dto[...] = dto[...] - dot_parts(split(full_ref[:, own_at]), product, ((0,), (0,)))
        uto[...] = -dot_parts(split(u[...]), product, INNER)

    def right_source(product_ref, f, sto):
        sto[...] = sto[...] - dot3(f[...], product_ref[...])

    c_do = copy(DO, d_ref.at[1], "partner")
    c_uo = copy(UO, u_ref.at[1], "partner")
    c_eo = copy(EO, u_ref.at[0], "partner")
    c_e = copy(EB, u_ref.at[0], "below")
    c_ex = copy(EX, bufs.at[EB], "partner")
    c_ulr = copy(ULR, u_ref.at[1], "over")
    c_flr = copy(FLR, f_ref.at[1], "over")
    c_ulf = copy(UL, bufs.at[ULR], "below")
    top, low = slice(0, half // 2), slice(half // 2, half)
    c_flf = [
        copy(FL, bufs.at[FLR, top], "below", bufs.at[FL, top]),
        copy(FL2, bufs.at[FLR, low], "below", bufs.at[FL, low]),
    ]
    c_fb = copy(FB, cur.at[2], "below")
    c_do1 = copy(DO1, cur.at[0], "partner")
    c_uo1 = copy(UO1, cur.at[1], "partner")
    c_uao = copy(UAO, fresh_ref.at[0], "partner")
    c_ul1 = copy(UL1, fresh_ref.at[0], "over")
    c_fl1 = copy(FL1, fresh_ref.at[1], "over")
    c_ru = copy(RU, fresh_ref.at[0], "above", uout_ref.at[0])
    c_rf = copy(RF, fresh_ref.at[1], "above", fout_ref.at[0])
    c_zlr = copy_tiles(ZLR, ztiles.at[0], "over")
    c_zl = copy_tiles(ZL, zbufs.at[ZLR], "below")
    c_zlo = copy_tiles(ZLO, zbufs.at[ZL], "partner")
    c_za = copy_tiles(ZA, ztiles.at[1], "below")
    c_zao = copy_tiles(ZAO, zbufs.at[ZA], "partner")
    c_zl1 = copy_tiles(ZL1, zbufs.at[ZA], "over")
    c_zl1o = copy_tiles(ZL1O, zbufs.at[ZL1], "partner")

    c_do.start()
    pl.when(odd)(c_e.start)

    pl.when(odd_over)(c_ulr.start)
    c_uo.start()
    c_eo.start()
    fill_own(d_ref.at[1])

    def ready():
        c_do.wait_recv()
        fill_other(bufs.at[DO])

    def after(k):
        pl.when(jnp.logical_and(odd_over, k == 2))(c_flr.start)

        @pl.when(jnp.logical_and(odd_under, k == 2))
        def _():
            c_ulr.wait_recv()
            c_ulf.start()

    invert(s_ref, tile_ref, fac_ref, col_ref, ready, send_factor, after)

    @pl.when(odd_over)
    def _():
        pack(ztiles.at[0])
        for i in c_zlr:
            i.start()

    store_inverse()
    c_uo.wait_recv()
    left(
        u_ref.at[1], bufs.at[UO], f_ref.at[1], d_ref.at[0], f_ref.at[0], cur.at[0], cur.at[2], scaled_ref
    )
    c_eo.wait_recv()
    dout_ref[1] = d_ref[1]
    uout_ref[1] = u_ref[1]
    fout_ref[1] = f_ref[1]

    @pl.when(odd)
    def _():
        c_fb.start()
        full_ref[:half] = u_ref[0]
        full_ref[half:] = bufs[EO]
        right_block(cur.at[0])
        c_do1.start()
        fill_own(cur.at[0])

        def ready():
            c_do1.wait_recv()
            fill_other(bufs.at[DO1])
            dout_ref[0] = cur[0]

            @pl.when(odd_under)
            def _():
                for arriving, sent in zip(c_zlr, c_zl):
                    arriving.wait_recv()
                    sent.start()

        def after(k):
            @pl.when(jnp.logical_and(odd_under, k == 1))
            def _():
                c_flr.wait_recv()
                c_flf[0].start()

        invert(s_ref, tile_ref, fac_ref, col_ref, ready, lambda k: None, after)
        pack(ztiles.at[1])
        for i in c_za:
            i.start()
        pl.when(odd_under)(c_flf[1].start)
        c_ru.wait_recv()
        c_rf.wait_recv()

    @pl.when(even)
    def _():
        c_e.wait_recv()
        c_ex.start()
        c_ex.wait_recv()
        assemble(onward_ref, bufs.at[EB], bufs.at[EX])
        fresh_ref[0] = -dot3(scaled_ref[0], onward_ref[...])
        c_ru.start()
        c_uao.start()
        pl.when(even_right)(c_ul1.start)
        c_fb.wait_recv()
        fresh_ref[1] = bufs[FB] - dot3(scaled_ref[1], onward_ref[...])
        c_rf.start()
        pl.when(even_right)(c_fl1.start)
        cur[1] = u_ref[0]

        @pl.when(has_left)
        def _():
            receive(ZL, ZLO, c_zl, c_zlo)
            assemble(full_ref, u_ref.at[0], bufs.at[EO])
            ahead(ahead_ref)
            c_ulf.wait_recv()
            right(ahead_ref, bufs.at[UL], cur.at[0], cur.at[1])

        c_uo1.start()
        c_uo1.wait_recv()
        assemble(full_ref, cur.at[1], bufs.at[UO1])
        uout_ref[0] = cur[1]
        c_uao.wait_recv()
        receive(ZA, ZAO, c_za, c_zao, c_zl1, even_right)
        left(
            fresh_ref.at[0], bufs.at[UAO], fresh_ref.at[1], cur.at[0], cur.at[2], dout_ref.at[0], fout_ref.at[0]
        )

    @pl.when(even_left)
    def _():
        receive(ZL1, ZL1O, c_zl1, c_zl1o)
        ahead(onward_ref)
        c_ul1.wait_recv()
        right(onward_ref, bufs.at[UL1], dout_ref.at[0], uout_ref.at[0])
        c_fl1.wait_recv()
        right_source(onward_ref, bufs.at[FL1], fout_ref.at[0])
        for arriving, rows in zip(c_flf, (top, low)):
            arriving.wait_recv()
            right_source(ahead_ref, bufs.at[FL, rows], fout_ref.at[0, rows])

    def drained(condition, copies):
        @pl.when(condition)
        def _():
            for i in copies:
                i.wait_send()

    for i in (c_do, c_uo, c_eo):
        i.wait_send()
    drained(odd_over, [c_ulr, c_flr] + c_zlr)
    drained(odd_under, [c_ulf] + c_flf + c_zl)
    drained(even_left, c_zlo)
    drained(even, [copy_factor(k, c) for k in range(blocks) for c in range(k, blocks)])
    drained(odd, [c_e, c_fb, c_do1] + c_za)
    drained(even, [c_ex, c_ru, c_rf, c_uao, c_uo1] + c_zao)
    drained(even_right, [c_ul1, c_fl1] + c_zl1)
    drained(even_left, c_zl1o)


SLOTS = 18
DO, UO, EO, EB, EX, ULR, FLR, UL, FL, FB, DO1, UO1, UAO, UL1, FL1, FL2, RU, RF = range(SLOTS)
ZSLOTS = 7
ZLR, ZL, ZLO, ZA, ZAO, ZL1, ZL1O = range(ZSLOTS)
ZTILES = 5


def body(tm_size, diagonal_blocks, upper_blocks, right_sides):
    shape = diagonal_blocks.shape
    half, size = shape[1], shape[2]
    tile, blocks = half // 2, size // TILE
    whole = pl.BlockSpec(memory_space=pltpu.VMEM)
    return pl.pallas_call(
        functools.partial(kernel, tm_size),
        out_shape=[jax.ShapeDtypeStruct(shape, F32)] * 3,
        in_specs=[whole] * 3,
        out_specs=[whole] * 3,
        scratch_shapes=[
            pltpu.VMEM((size, size), F32),
            pltpu.VMEM((TILE, TILE), F32),
            pltpu.VMEM((blocks, blocks, TILE, TILE), F32),
            pltpu.VMEM((blocks - 1, TILE, TILE), F32),
            pltpu.VMEM((size, size), F32),
            pltpu.VMEM((size, size), F32),
            pltpu.VMEM((size, size), F32),
            pltpu.VMEM((size, size), F32),
            pltpu.VMEM((3, half, size), F32),
            pltpu.VMEM((2, half, size), F32),
            pltpu.VMEM((2, half, size), F32),
            pltpu.VMEM((2, ZTILES, tile, tile), F32),
            pltpu.VMEM((FL2, half, size), F32),
            pltpu.VMEM((ZSLOTS, ZTILES, tile, tile), F32),
            pltpu.VMEM((blocks, blocks, TILE, TILE), F32),
            pltpu.SemaphoreType.DMA((SLOTS,)),
            pltpu.SemaphoreType.DMA((SLOTS,)),
            pltpu.SemaphoreType.DMA((ZSLOTS * ZTILES,)),
            pltpu.SemaphoreType.DMA((ZSLOTS * ZTILES,)),
            pltpu.SemaphoreType.DMA((blocks * blocks,)),
            pltpu.SemaphoreType.DMA((blocks * blocks,)),
        ],
        compiler_params=pltpu.CompilerParams(
            vmem_limit_bytes=50 * 2**20, collective_id=0, has_side_effects=True
        ),
        name="reduce_levels",
    )(diagonal_blocks, upper_blocks, right_sides)


def solution(mesh):
    placed = (P("tm", "col", None),) * 3
    return jax.shard_map(
        functools.partial(body, mesh.shape["tm"]),
        mesh=mesh,
        in_specs=placed,
        out_specs=placed,
        check_vma=False,
    )
```

```python
import functools

import jax
import jax.numpy as jnp
from jax import lax
from jax.experimental import pallas as pl
from jax.experimental.pallas import tpu as pltpu
from jax.sharding import PartitionSpec as P

LEVELS = 2
TILE = 128
PANEL = 8
F32 = jnp.float32
BF16 = jnp.bfloat16


def split(values):
    high = values.astype(BF16)
    return high, (values - high.astype(F32)).astype(BF16)


def dot_parts(left, right, dims):
    def one(a, b):
        return lax.dot_general(a, b, (dims, ((), ())), preferred_element_type=F32)

    return one(left[0], right[0]) + (one(left[0], right[1]) + one(left[1], right[0]))


def dot3(left, right, dims=((1,), (0,))):
    return dot_parts(split(left), split(right), dims)


def panel_step(a, p):
    size = a[0].shape[1]
    count = size // PANEL
    base = PANEL * p
    lanes = lax.broadcasted_iota(jnp.int32, (PANEL, size), 1)
    subs = lax.broadcasted_iota(jnp.int32, (PANEL, size), 0)
    inside = jnp.logical_and(lanes >= base, lanes < base + PANEL)

    def spread(values, i):
        return jnp.broadcast_to(values[:, base + i : base + i + 1], (PANEL, size))

    head = [spread(a[p], i) for i in range(PANEL)]
    s = [
        [jnp.broadcast_to(head[j][i : i + 1, :], (PANEL, size)) if j >= i else None for j in range(PANEL)]
        for i in range(PANEL)
    ]
    rows = [
        jnp.where(
            inside,
            jnp.where(lanes == base + i, 1.0, 0.0),
            jnp.broadcast_to(a[p][i : i + 1, :], (PANEL, size)),
        )
        for i in range(PANEL)
    ]
    scale = [None] * PANEL
    low = {}
    for k in range(PANEL):
        scale[k] = 1.0 / s[k][k]
        for i in range(k + 1, PANEL):
            low[i, k] = s[k][i] * scale[k]
            for j in range(i, PANEL):
                s[i][j] = s[i][j] - low[i, k] * s[k][j]
            rows[i] = rows[i] - low[i, k] * rows[k]
    for k in range(PANEL):
        rows[k] = rows[k] * scale[k]
    for k in range(PANEL - 1, 0, -1):
        for i in range(k):
            rows[i] = rows[i] - low[k, i] * rows[k]
    solved = rows[0]
    for i in range(1, PANEL):
        solved = jnp.where(subs == i, rows[i], solved)
    fresh = [None] * count
    fresh[p] = solved
    for step in range(1, count):
        g = (p + step) % count
        col = [spread(a[g], i) for i in range(PANEL)]
        terms = [col[i] * rows[i] for i in range(PANEL)]
        while len(terms) > 1:
            terms = [terms[i] + terms[i + 1] for i in range(0, len(terms), 2)]
        fresh[g] = jnp.where(inside, 0.0, a[g]) - terms[0]
    return fresh


INNER = ((1,), (0,))
OUTER = ((1,), (1,))


def invert(s_ref, tile_ref, fac_ref, col_ref, ready, send, after):
    blocks = s_ref.shape[0] // TILE
    steps = TILE // PANEL

    def span(index):
        return pl.ds(pl.multiple_of(index * TILE, TILE), TILE)

    def fixed(index):
        return slice(index * TILE, (index + 1) * TILE)

    def take_column(k):
        for o in range(blocks - 1):
            rat = span(lax.rem(k + o + 1, blocks))
            col_ref[o] = s_ref[rat, span(k)]
            s_ref[rat, span(k)] = jnp.zeros((TILE, TILE), F32)

    def row_job(k, c):
        inverse = tile_ref[...]
        value = jnp.where(k == c, inverse, dot3(inverse, s_ref[span(k), fixed(c)]))
        fac_ref[k, c] = value
        s_ref[span(k), fixed(c)] = value

    def update_job(k, o, c):
        rat = span(lax.rem(k + o + 1, blocks))
        s_ref[rat, fixed(c)] = s_ref[rat, fixed(c)] - dot3(col_ref[o], fac_ref[k, c])

    def invert_tile(k, jobs):
        groups = [
            s_ref[pl.ds(pl.multiple_of(k * TILE, TILE) + PANEL * g, PANEL), span(k)] for g in range(steps)
        ]
        for p in range(steps):
            groups = panel_step(groups, p)
            for job in jobs[p * len(jobs) // steps : (p + 1) * len(jobs) // steps]:
                job()
        for g in range(steps):
            tile_ref[PANEL * g : PANEL * (g + 1), :] = groups[g]

    invert_tile(0, [])
    ready()

    @pl.loop(1, blocks)
    def _(k):
        last = k - 1
        take_column(last)
        row = dot3(tile_ref[...], s_ref[span(last), span(k)])
        s_ref[span(k), span(k)] = s_ref[span(k), span(k)] - dot3(col_ref[0], row)
        jobs = [functools.partial(row_job, last, c) for c in range(blocks)]
        jobs.append(lambda: send(last))
        for o in range(blocks - 1):
            jobs += [functools.partial(update_job, last, o, c) for c in range(blocks)]
        invert_tile(k, jobs)
        after(k)

    end = blocks - 1
    fac_ref[end, end] = tile_ref[...]
    send(end)
    take_column(end)
    s_ref[fixed(end), fixed(end)] = tile_ref[...]
    for c in range(end):
        row_job(end, c)
    for o in range(blocks - 1):
        for c in range(blocks):
            update_job(end, o, c)


def kernel(
    tm_size, d_ref, u_ref, f_ref, dout_ref, uout_ref, fout_ref,
    s_ref, tile_ref, fac_ref, col_ref, z_ref, full_ref, onward_ref, ahead_ref, cur, scaled_ref, fresh_ref, ztiles, bufs, zbufs, fbufs,
    send_sem, recv_sem, zsend_sem, zrecv_sem, fsend_sem, frecv_sem,
):
    half, size = d_ref.shape[1], d_ref.shape[2]
    column = lax.axis_index("col")
    place = lax.axis_index("tm")
    above, below = lax.rem(place + 1, tm_size), lax.rem(place + tm_size - 1, tm_size)
    over, under = lax.rem(place + 2, tm_size), lax.rem(place + tm_size - 2, tm_size)
    partner = 1 - column
    odd = lax.rem(place, 2) == 1
    even = lax.rem(place, 2) == 0
    has_left = place > 0
    has_right = place < tm_size - 1
    has_under, has_over = place > 1, place < tm_size - 2
    odd_over = jnp.logical_and(odd, has_over)
    odd_under = jnp.logical_and(odd, has_under)
    even_left = jnp.logical_and(even, has_under)
    even_right = jnp.logical_and(even, has_over)
    own_at = pl.ds(pl.multiple_of(column * half, half), half)
    other_at = pl.ds(pl.multiple_of(partner * half, half), half)
    tile = half // 2

    barrier = pltpu.get_barrier_semaphore()

    def greet(where):
        pl.semaphore_signal(barrier, inc=1, device_id=where, device_id_type=pl.DeviceIdType.MESH)

    greet((place, partner))
    pl.when(has_left)(lambda: greet((below, column)))
    pl.when(has_right)(lambda: greet((above, column)))
    pl.when(has_under)(lambda: greet((under, column)))
    pl.when(has_over)(lambda: greet((over, column)))
    peers = [x.astype(jnp.int32) for x in (has_left, has_right, has_under, has_over)]
    pl.semaphore_wait(barrier, 1 + peers[0] + peers[1] + peers[2] + peers[3])

    targets = {"above": (above, column), "below": (below, column), "partner": (place, partner), "over": (over, column)}

    def copy(slot, source, target, landing=None):
        return pltpu.make_async_remote_copy(
            src_ref=source, dst_ref=bufs.at[slot] if landing is None else landing,
            send_sem=send_sem.at[slot], recv_sem=recv_sem.at[slot],
            device_id=targets[target], device_id_type=pl.DeviceIdType.MESH,
        )

    def copy_tiles(slot, source, target):
        return [
            pltpu.make_async_remote_copy(
                src_ref=source.at[i], dst_ref=zbufs.at[slot, i],
                send_sem=zsend_sem.at[ZTILES * slot + i], recv_sem=zrecv_sem.at[ZTILES * slot + i],
                device_id=targets[target], device_id_type=pl.DeviceIdType.MESH,
            )
            for i in range(ZTILES)
        ]

    def assemble(into, own, other):
        into[own_at, :] = own[...]
        into[other_at, :] = other[...]

    def tile_places(c):
        def at(row):
            return pl.ds(pl.multiple_of(row, tile), tile)

        first, far = c * half, (1 - c) * half
        near = [at(first), at(first + tile)]
        return [
            (near[0], near[0]), (near[0], near[1]), (near[1], near[1]),
            (near[0], at(far + c * tile)), (near[1], at(far + (1 - c) * tile)),
        ]

    def pack(into):
        places = [(0, 0), (0, tile), (tile, tile), (0, half + column * tile), (tile, half + partner * tile)]
        for i, (row, col) in enumerate(places):
            into[i] = s_ref[row : row + tile, pl.ds(pl.multiple_of(col, tile), tile)]

    def fill_own(source):
        s_ref[:half, :half] = source[:, own_at]
        s_ref[:half, half:] = source[:, other_at]

    def fill_other(source):
        s_ref[half:, :half] = source[:, own_at]
        s_ref[half:, half:] = source[:, other_at]

    def store_inverse():
        z_ref[own_at, own_at] = s_ref[:half, :half]
        z_ref[own_at, other_at] = s_ref[:half, half:]
        z_ref[other_at, own_at] = s_ref[half:, :half]
        z_ref[other_at, other_at] = s_ref[half:, half:]

    blocks = size // TILE

    def copy_factor(k, c):
        sem = k * blocks + c
        return pltpu.make_async_remote_copy(
            src_ref=fac_ref.at[k, c], dst_ref=fbufs.at[k, c],
            send_sem=fsend_sem.at[sem], recv_sem=frecv_sem.at[sem],
            device_id=targets["above"], device_id_type=pl.DeviceIdType.MESH,
        )

    def send_factor(k):
        for c in range(blocks):
            pl.when(jnp.logical_and(even, c >= k))(copy_factor(k, c).start)

    def unpack(slot, c):
        for i, (row, col) in enumerate(tile_places(c)):
            value = zbufs[slot, i]
            z_ref[row, col] = value
            if i not in (0, 2):
                z_ref[col, row] = value.T

    def receive(slot, other_slot, arriving, shared, onward=None, condition=None):
        for i in range(ZTILES):
            arriving[i].wait_recv()
            shared[i].start()
            if onward is not None:
                pl.when(condition)(onward[i].start)
        unpack(slot, column)
        for i in range(ZTILES):
            shared[i].wait_recv()
        unpack(other_slot, partner)

    def left(u, uother, f, d, s, dto, sto, keep=None):
        z = split(z_ref[...])
        own, other = split(u[...]), split(uother[...])
        for n, (values, base, out) in enumerate(((own, d, dto), (split(f[...]), s, sto))):
            scaled = dot_parts(values, z, INNER)
            if keep is not None:
                keep[n] = scaled
            scaled = split(scaled)
            out[:, own_at] = base[:, own_at] - dot_parts(scaled, own, OUTER)
            out[:, other_at] = base[:, other_at] - dot_parts(scaled, other, OUTER)

    def right_block(dto):
        for m in range(blocks):
            at = slice(m * TILE, (m + 1) * TILE)
            for c in range(m, blocks):
                copy_factor(m, c).wait_recv()
            onward_ref[at] = dot3(fbufs[m, m], full_ref[at])
            for c in range(m + 1, blocks):
                rat = slice(c * TILE, (c + 1) * TILE)
                full_ref[rat] = full_ref[rat] - dot3(fbufs[m, c], full_ref[at], ((0,), (0,)))
        dto[...] = dto[...] - dot3(full_ref[:, own_at], onward_ref[...], ((0,), (0,)))

    def ahead(into):
        into[...] = dot3(z_ref[...], full_ref[...])

    def right(product_ref, u, dto, uto):
        product = split(product_ref[...])
        dto[...] = dto[...] - dot_parts(split(full_ref[:, own_at]), product, ((0,), (0,)))
        uto[...] = -dot_parts(split(u[...]), product, INNER)

    def right_source(product_ref, f, sto):
        sto[...] = sto[...] - dot3(f[...], product_ref[...])

    def keep():
        dout_ref[1] = d_ref[1]
        uout_ref[1] = u_ref[1]
        fout_ref[1] = f_ref[1]

    c_do = copy(DO, d_ref.at[1], "partner")
    c_uo = copy(UO, u_ref.at[1], "partner")
    c_eo = copy(EO, u_ref.at[0], "partner")
    c_e = copy(EB, u_ref.at[0], "below")
    c_ex = copy(EX, bufs.at[EB], "partner")
    c_ulr = copy(ULR, u_ref.at[1], "over")
    c_flr = copy(FLR, f_ref.at[1], "over")
    c_ulf = copy(UL, bufs.at[ULR], "below")
    top, low = slice(0, half // 2), slice(half // 2, half)
    c_flf = [
        copy(FL, bufs.at[FLR, top], "below", bufs.at[FL, top]),
        copy(FL2, bufs.at[FLR, low], "below", bufs.at[FL, low]),
    ]
    c_fb = copy(FB, cur.at[2], "below")
    c_do1 = copy(DO1, cur.at[0], "partner")
    c_uo1 = copy(UO1, cur.at[1], "partner")
    c_uao = copy(UAO, fresh_ref.at[0], "partner")
    c_ul1 = copy(UL1, fresh_ref.at[0], "over")
    c_fl1 = copy(FL1, fresh_ref.at[1], "over")
    c_ru = copy(RU, fresh_ref.at[0], "above", uout_ref.at[0])
    c_rf = copy(RF, fresh_ref.at[1], "above", fout_ref.at[0])
    c_zlr = copy_tiles(ZLR, ztiles.at[0], "over")
    c_zl = copy_tiles(ZL, zbufs.at[ZLR], "below")
    c_zlo = copy_tiles(ZLO, zbufs.at[ZL], "partner")
    c_za = copy_tiles(ZA, ztiles.at[1], "below")
    c_zao = copy_tiles(ZAO, zbufs.at[ZA], "partner")
    c_zl1 = copy_tiles(ZL1, zbufs.at[ZA], "over")
    c_zl1o = copy_tiles(ZL1O, zbufs.at[ZL1], "partner")

    c_do.start()
    pl.when(odd)(c_e.start)

    pl.when(odd_over)(c_ulr.start)
    c_uo.start()
    c_eo.start()
    fill_own(d_ref.at[1])

    def ready():
        c_do.wait_recv()
        fill_other(bufs.at[DO])

    def send(k):
        send_factor(k)
        pl.when(jnp.logical_and(odd_over, k == 1))(c_flr.start)

        @pl.when(jnp.logical_and(odd_under, k == 1))
        def _():
            c_ulr.wait_recv()
            c_ulf.start()

    invert(s_ref, tile_ref, fac_ref, col_ref, ready, send, lambda k: None)

    @pl.when(odd_over)
    def _():
        pack(ztiles.at[0])
        for i in c_zlr:
            i.start()

    store_inverse()
    c_uo.wait_recv()
    left(
        u_ref.at[1], bufs.at[UO], f_ref.at[1], d_ref.at[0], f_ref.at[0], cur.at[0], cur.at[2], scaled_ref
    )
    c_eo.wait_recv()

    @pl.when(odd)
    def _():
        c_fb.start()
        full_ref[:half] = u_ref[0]
        full_ref[half:] = bufs[EO]
        right_block(cur.at[0])
        c_do1.start()
        fill_own(cur.at[0])

        def ready():
            c_do1.wait_recv()
            fill_other(bufs.at[DO1])
            dout_ref[0] = cur[0]

            @pl.when(odd_under)
            def _():
                for arriving, sent in zip(c_zlr, c_zl):
                    arriving.wait_recv()
                    sent.start()

        def after(k):
            @pl.when(jnp.logical_and(odd_under, k == 1))
            def _():
                c_flr.wait_recv()
                c_flf[0].start()

        invert(s_ref, tile_ref, fac_ref, col_ref, ready, lambda k: None, after)
        pack(ztiles.at[1])
        for n, i in enumerate(c_za):
            i.start()
            if n > 0:
                c_za[n - 1].wait_send()
        c_za[-1].wait_send()
        pl.when(odd_under)(c_flf[1].start)
        keep()
        c_ru.wait_recv()
        c_rf.wait_recv()

    @pl.when(even)
    def _():
        c_e.wait_recv()
        c_ex.start()
        c_ex.wait_recv()
        assemble(onward_ref, bufs.at[EB], bufs.at[EX])
        fresh_ref[0] = -dot3(scaled_ref[0], onward_ref[...])
        c_ru.start()
        c_uao.start()
        pl.when(even_right)(c_ul1.start)
        c_fb.wait_recv()
        fresh_ref[1] = bufs[FB] - dot3(scaled_ref[1], onward_ref[...])
        c_rf.start()
        pl.when(even_right)(c_fl1.start)
        cur[1] = u_ref[0]

        @pl.when(has_left)
        def _():
            receive(ZL, ZLO, c_zl, c_zlo)
            assemble(full_ref, u_ref.at[0], bufs.at[EO])
            ahead(ahead_ref)
            c_ulf.wait_recv()
            right(ahead_ref, bufs.at[UL], cur.at[0], cur.at[1])

        c_uo1.start()
        keep()
        c_uo1.wait_recv()
        assemble(full_ref, cur.at[1], bufs.at[UO1])
        uout_ref[0] = cur[1]
        c_uao.wait_recv()

        @pl.when(has_left)
        def _():
            c_flf[0].wait_recv()
            right_source(ahead_ref, bufs.at[FL, top], cur.at[2, top])

        receive(ZA, ZAO, c_za, c_zao, c_zl1, even_right)
        left(
            fresh_ref.at[0], bufs.at[UAO], fresh_ref.at[1], cur.at[0], cur.at[2], dout_ref.at[0], fout_ref.at[0]
        )

    @pl.when(even_left)
    def _():
        receive(ZL1, ZL1O, c_zl1, c_zl1o)
        ahead(onward_ref)
        c_ul1.wait_recv()
        right(onward_ref, bufs.at[UL1], dout_ref.at[0], uout_ref.at[0])
        c_fl1.wait_recv()
        right_source(onward_ref, bufs.at[FL1], fout_ref.at[0])
        c_flf[1].wait_recv()
        right_source(ahead_ref, bufs.at[FL, low], fout_ref.at[0, low])

    def drained(condition, copies):
        @pl.when(condition)
        def _():
            for i in copies:
                i.wait_send()

    for i in (c_do, c_uo, c_eo):
        i.wait_send()
    drained(odd_over, [c_ulr, c_flr] + c_zlr)
    drained(odd_under, [c_ulf] + c_flf + c_zl)
    drained(even_left, c_zlo)
    drained(even, [copy_factor(k, c) for k in range(blocks) for c in range(k, blocks)])
    drained(odd, [c_e, c_fb, c_do1])
    drained(even, [c_ex, c_ru, c_rf, c_uao, c_uo1] + c_zao)
    drained(even_right, [c_ul1, c_fl1] + c_zl1)
    drained(even_left, c_zl1o)


SLOTS = 18
DO, UO, EO, EB, EX, ULR, FLR, UL, FL, FB, DO1, UO1, UAO, UL1, FL1, FL2, RU, RF = range(SLOTS)
ZSLOTS = 7
ZLR, ZL, ZLO, ZA, ZAO, ZL1, ZL1O = range(ZSLOTS)
ZTILES = 5


def body(tm_size, diagonal_blocks, upper_blocks, right_sides):
    shape = diagonal_blocks.shape
    half, size = shape[1], shape[2]
    tile, blocks = half // 2, size // TILE
    whole = pl.BlockSpec(memory_space=pltpu.VMEM)
    return pl.pallas_call(
        functools.partial(kernel, tm_size),
        out_shape=[jax.ShapeDtypeStruct(shape, F32)] * 3,
        in_specs=[whole] * 3,
        out_specs=[whole] * 3,
        scratch_shapes=[
            pltpu.VMEM((size, size), F32),
            pltpu.VMEM((TILE, TILE), F32),
            pltpu.VMEM((blocks, blocks, TILE, TILE), F32),
            pltpu.VMEM((blocks - 1, TILE, TILE), F32),
            pltpu.VMEM((size, size), F32),
            pltpu.VMEM((size, size), F32),
            pltpu.VMEM((size, size), F32),
            pltpu.VMEM((size, size), F32),
            pltpu.VMEM((3, half, size), F32),
            pltpu.VMEM((2, half, size), F32),
            pltpu.VMEM((2, half, size), F32),
            pltpu.VMEM((2, ZTILES, tile, tile), F32),
            pltpu.VMEM((FL2, half, size), F32),
            pltpu.VMEM((ZSLOTS, ZTILES, tile, tile), F32),
            pltpu.VMEM((blocks, blocks, TILE, TILE), F32),
            pltpu.SemaphoreType.DMA((SLOTS,)),
            pltpu.SemaphoreType.DMA((SLOTS,)),
            pltpu.SemaphoreType.DMA((ZSLOTS * ZTILES,)),
            pltpu.SemaphoreType.DMA((ZSLOTS * ZTILES,)),
            pltpu.SemaphoreType.DMA((blocks * blocks,)),
            pltpu.SemaphoreType.DMA((blocks * blocks,)),
        ],
        compiler_params=pltpu.CompilerParams(
            vmem_limit_bytes=50 * 2**20, collective_id=0, has_side_effects=True
        ),
        name="reduce_levels",
    )(diagonal_blocks, upper_blocks, right_sides)


def solution(mesh):
    placed = (P("tm", "col", None),) * 3
    return jax.shard_map(
        functools.partial(body, mesh.shape["tm"]),
        mesh=mesh,
        in_specs=placed,
        out_specs=placed,
        check_vma=False,
    )
```

```python
import functools

import jax
import jax.numpy as jnp
from jax import lax
from jax.experimental import pallas as pl
from jax.experimental.pallas import tpu as pltpu
from jax.sharding import PartitionSpec as P

LEVELS = 2
TILE = 128
PANEL = 8
F32 = jnp.float32
BF16 = jnp.bfloat16


def split(values):
    high = values.astype(BF16)
    return high, (values - high.astype(F32)).astype(BF16)


def dot_parts(left, right, dims):
    def one(a, b):
        return lax.dot_general(a, b, (dims, ((), ())), preferred_element_type=F32)

    return one(left[0], right[0]) + (one(left[0], right[1]) + one(left[1], right[0]))


def dot3(left, right, dims=((1,), (0,))):
    return dot_parts(split(left), split(right), dims)


def panel_step(a, p):
    size = a[0].shape[1]
    count = size // PANEL
    base = PANEL * p
    lanes = lax.broadcasted_iota(jnp.int32, (PANEL, size), 1)
    subs = lax.broadcasted_iota(jnp.int32, (PANEL, size), 0)
    inside = jnp.logical_and(lanes >= base, lanes < base + PANEL)

    def spread(values, i):
        return jnp.broadcast_to(values[:, base + i : base + i + 1], (PANEL, size))

    head = [spread(a[p], i) for i in range(PANEL)]
    s = [
        [jnp.broadcast_to(head[j][i : i + 1, :], (PANEL, size)) if j >= i else None for j in range(PANEL)]
        for i in range(PANEL)
    ]
    rows = [
        jnp.where(
            inside,
            jnp.where(lanes == base + i, 1.0, 0.0),
            jnp.broadcast_to(a[p][i : i + 1, :], (PANEL, size)),
        )
        for i in range(PANEL)
    ]
    scale = [None] * PANEL
    low = {}
    for k in range(PANEL):
        scale[k] = 1.0 / s[k][k]
        for i in range(k + 1, PANEL):
            low[i, k] = s[k][i] * scale[k]
            for j in range(i, PANEL):
                s[i][j] = s[i][j] - low[i, k] * s[k][j]
            rows[i] = rows[i] - low[i, k] * rows[k]
    for k in range(PANEL):
        rows[k] = rows[k] * scale[k]
    for k in range(PANEL - 1, 0, -1):
        for i in range(k):
            rows[i] = rows[i] - low[k, i] * rows[k]
    solved = rows[0]
    for i in range(1, PANEL):
        solved = jnp.where(subs == i, rows[i], solved)
    fresh = [None] * count
    fresh[p] = solved
    for step in range(1, count):
        g = (p + step) % count
        col = [spread(a[g], i) for i in range(PANEL)]
        terms = [col[i] * rows[i] for i in range(PANEL)]
        while len(terms) > 1:
            terms = [terms[i] + terms[i + 1] for i in range(0, len(terms), 2)]
        fresh[g] = jnp.where(inside, 0.0, a[g]) - terms[0]
    return fresh


INNER = ((1,), (0,))
OUTER = ((1,), (1,))


def invert(s_ref, tile_ref, fac_ref, col_ref, ready, send, after):
    blocks = s_ref.shape[0] // TILE
    steps = TILE // PANEL

    def span(index):
        return pl.ds(pl.multiple_of(index * TILE, TILE), TILE)

    def fixed(index):
        return slice(index * TILE, (index + 1) * TILE)

    def take_column(k):
        for o in range(blocks - 1):
            rat = span(lax.rem(k + o + 1, blocks))
            col_ref[o] = s_ref[rat, span(k)]
            s_ref[rat, span(k)] = jnp.zeros((TILE, TILE), F32)

    def row_job(k, c):
        inverse = tile_ref[...]
        value = jnp.where(k == c, inverse, dot3(inverse, s_ref[span(k), fixed(c)]))
        fac_ref[k, c] = value
        s_ref[span(k), fixed(c)] = value

    def update_job(k, o, c):
        rat = span(lax.rem(k + o + 1, blocks))
        s_ref[rat, fixed(c)] = s_ref[rat, fixed(c)] - dot3(col_ref[o], fac_ref[k, c])

    def invert_tile(k, jobs):
        groups = [
            s_ref[pl.ds(pl.multiple_of(k * TILE, TILE) + PANEL * g, PANEL), span(k)] for g in range(steps)
        ]
        for p in range(steps):
            groups = panel_step(groups, p)
            for job in jobs[p * len(jobs) // steps : (p + 1) * len(jobs) // steps]:
                job()
        for g in range(steps):
            tile_ref[PANEL * g : PANEL * (g + 1), :] = groups[g]

    invert_tile(0, [])
    ready()

    @pl.loop(1, blocks)
    def _(k):
        last = k - 1
        take_column(last)
        row = dot3(tile_ref[...], s_ref[span(last), span(k)])
        s_ref[span(k), span(k)] = s_ref[span(k), span(k)] - dot3(col_ref[0], row)
        jobs = [functools.partial(row_job, last, c) for c in range(blocks)]
        jobs.append(lambda: send(last))
        for o in range(blocks - 1):
            jobs += [functools.partial(update_job, last, o, c) for c in range(blocks)]
        invert_tile(k, jobs)
        after(k)

    end = blocks - 1
    fac_ref[end, end] = tile_ref[...]
    send(end)
    take_column(end)
    s_ref[fixed(end), fixed(end)] = tile_ref[...]
    for c in range(end):
        row_job(end, c)
    for o in range(blocks - 1):
        for c in range(blocks):
            update_job(end, o, c)


def kernel(
    tm_size, d_ref, u_ref, f_ref, dout_ref, uout_ref, fout_ref,
    s_ref, tile_ref, fac_ref, col_ref, z_ref, full_ref, onward_ref, ahead_ref, cur, scaled_ref, fresh_ref, ztiles, bufs, zbufs, fbufs,
    send_sem, recv_sem, zsend_sem, zrecv_sem, fsend_sem, frecv_sem,
):
    half, size = d_ref.shape[1], d_ref.shape[2]
    column = lax.axis_index("col")
    place = lax.axis_index("tm")
    above, below = lax.rem(place + 1, tm_size), lax.rem(place + tm_size - 1, tm_size)
    over, under = lax.rem(place + 2, tm_size), lax.rem(place + tm_size - 2, tm_size)
    partner = 1 - column
    odd = lax.rem(place, 2) == 1
    even = lax.rem(place, 2) == 0
    has_left = place > 0
    has_right = place < tm_size - 1
    has_under, has_over = place > 1, place < tm_size - 2
    odd_over = jnp.logical_and(odd, has_over)
    odd_under = jnp.logical_and(odd, has_under)
    even_left = jnp.logical_and(even, has_under)
    even_right = jnp.logical_and(even, has_over)
    own_at = pl.ds(pl.multiple_of(column * half, half), half)
    other_at = pl.ds(pl.multiple_of(partner * half, half), half)
    tile = half // 2

    barrier = pltpu.get_barrier_semaphore()

    def greet(where):
        pl.semaphore_signal(barrier, inc=1, device_id=where, device_id_type=pl.DeviceIdType.MESH)

    greet((place, partner))
    pl.when(has_left)(lambda: greet((below, column)))
    pl.when(has_right)(lambda: greet((above, column)))
    pl.when(has_under)(lambda: greet((under, column)))
    pl.when(has_over)(lambda: greet((over, column)))
    peers = [x.astype(jnp.int32) for x in (has_left, has_right, has_under, has_over)]
    pl.semaphore_wait(barrier, 1 + peers[0] + peers[1] + peers[2] + peers[3])

    targets = {"above": (above, column), "below": (below, column), "partner": (place, partner), "over": (over, column)}

    def copy(slot, source, target, landing=None):
        return pltpu.make_async_remote_copy(
            src_ref=source, dst_ref=bufs.at[slot] if landing is None else landing,
            send_sem=send_sem.at[slot], recv_sem=recv_sem.at[slot],
            device_id=targets[target], device_id_type=pl.DeviceIdType.MESH,
        )

    def extent(i):
        return slice(0, tile + PANEL if i == 0 else tile)

    def copy_tiles(slot, source, target):
        return [
            pltpu.make_async_remote_copy(
                src_ref=source.at[i, extent(i)], dst_ref=zbufs.at[slot, i, extent(i)],
                send_sem=zsend_sem.at[ZTILES * slot + i], recv_sem=zrecv_sem.at[ZTILES * slot + i],
                device_id=targets[target], device_id_type=pl.DeviceIdType.MESH,
            )
            for i in range(ZTILES)
        ]

    def assemble(into, own, other):
        into[own_at, :] = own[...]
        into[other_at, :] = other[...]

    def tile_places(c):
        def at(row):
            return pl.ds(pl.multiple_of(row, tile), tile)

        first, far = c * half, (1 - c) * half
        near = [at(first), at(first + tile)]
        return near, [
            (near[0], near[1]), (near[0], at(far + c * tile)), (near[1], at(far + (1 - c) * tile)),
        ]

    down = lax.broadcasted_iota(jnp.int32, (tile, tile), 0)
    across = lax.broadcasted_iota(jnp.int32, (tile, tile), 1)

    def pack(into):
        first, second = s_ref[:tile, :tile], s_ref[tile:half, tile:half]
        into[0, :tile] = jnp.where(down > across, first, second)
        middle = jnp.sum(jnp.where(down == across, first, 0.0), axis=0, keepdims=True)
        into[0, tile:] = jnp.broadcast_to(middle, (PANEL, tile))
        places = [(0, tile), (0, half + column * tile), (tile, half + partner * tile)]
        for i, (row, col) in enumerate(places):
            into[1 + i, :tile] = s_ref[row : row + tile, pl.ds(pl.multiple_of(col, tile), tile)]

    def fill_own(source):
        s_ref[:half, :half] = source[:, own_at]
        s_ref[:half, half:] = source[:, other_at]

    def fill_other(source):
        s_ref[half:, :half] = source[:, own_at]
        s_ref[half:, half:] = source[:, other_at]

    def store_inverse():
        z_ref[own_at, own_at] = s_ref[:half, :half]
        z_ref[own_at, other_at] = s_ref[:half, half:]
        z_ref[other_at, own_at] = s_ref[half:, :half]
        z_ref[other_at, other_at] = s_ref[half:, half:]

    blocks = size // TILE

    def copy_factor(k, c):
        sem = k * blocks + c
        return pltpu.make_async_remote_copy(
            src_ref=fac_ref.at[k, c], dst_ref=fbufs.at[k, c],
            send_sem=fsend_sem.at[sem], recv_sem=frecv_sem.at[sem],
            device_id=targets["above"], device_id_type=pl.DeviceIdType.MESH,
        )

    def send_factor(k):
        for c in range(blocks):
            pl.when(jnp.logical_and(even, c >= k))(copy_factor(k, c).start)

    def unpack(slot, c):
        near, places = tile_places(c)
        both = zbufs[slot, 0, :tile]
        turned = both.T
        middle = jnp.broadcast_to(zbufs[slot, 0, tile : tile + 1], (tile, tile))
        z_ref[near[0], near[0]] = jnp.where(
            down > across, both, jnp.where(down < across, turned, middle)
        )
        z_ref[near[1], near[1]] = jnp.where(down > across, turned, both)
        for i, (row, col) in enumerate(places):
            value = zbufs[slot, 1 + i, :tile]
            z_ref[row, col] = value
            z_ref[col, row] = value.T

    def receive(slot, other_slot, arriving, shared, onward=None, condition=None):
        for i in range(ZTILES):
            arriving[i].wait_recv()
            shared[i].start()
            if onward is not None:
                pl.when(condition)(onward[i].start)
        unpack(slot, column)
        for i in range(ZTILES):
            shared[i].wait_recv()
        unpack(other_slot, partner)

    def left(u, uother, f, d, s, dto, sto, keep=None):
        z = split(z_ref[...])
        own, other = split(u[...]), split(uother[...])
        for n, (values, base, out) in enumerate(((own, d, dto), (split(f[...]), s, sto))):
            scaled = dot_parts(values, z, INNER)
            if keep is not None:
                keep[n] = scaled
            scaled = split(scaled)
            out[:, own_at] = base[:, own_at] - dot_parts(scaled, own, OUTER)
            out[:, other_at] = base[:, other_at] - dot_parts(scaled, other, OUTER)

    def right_block(dto):
        for m in range(blocks):
            at = slice(m * TILE, (m + 1) * TILE)
            for c in range(m, blocks):
                copy_factor(m, c).wait_recv()
            onward_ref[at] = dot3(fbufs[m, m], full_ref[at])
            for c in range(m + 1, blocks):
                rat = slice(c * TILE, (c + 1) * TILE)
                full_ref[rat] = full_ref[rat] - dot3(fbufs[m, c], full_ref[at], ((0,), (0,)))
        dto[...] = dto[...] - dot3(full_ref[:, own_at], onward_ref[...], ((0,), (0,)))

    def ahead(into):
        into[...] = dot3(z_ref[...], full_ref[...])

    def right(product_ref, u, dto, uto):
        product = split(product_ref[...])
        dto[...] = dto[...] - dot_parts(split(full_ref[:, own_at]), product, ((0,), (0,)))
        uto[...] = -dot_parts(split(u[...]), product, INNER)

    def right_source(product_ref, f, sto):
        sto[...] = sto[...] - dot3(f[...], product_ref[...])

    def keep():
        dout_ref[1] = d_ref[1]
        uout_ref[1] = u_ref[1]
        fout_ref[1] = f_ref[1]

    c_do = copy(DO, d_ref.at[1], "partner")
    c_uo = copy(UO, u_ref.at[1], "partner")
    c_eo = copy(EO, u_ref.at[0], "partner")
    c_e = copy(EB, u_ref.at[0], "below")
    c_ex = copy(EX, bufs.at[EB], "partner")
    c_ulr = copy(ULR, u_ref.at[1], "over")
    c_flr = copy(FLR, f_ref.at[1], "over")
    c_ulf = copy(UL, bufs.at[ULR], "below")
    top, low = slice(0, half // 2), slice(half // 2, half)
    c_flf = [
        copy(FL, bufs.at[FLR, top], "below", bufs.at[FL, top]),
        copy(FL2, bufs.at[FLR, low], "below", bufs.at[FL, low]),
    ]
    c_fb = copy(FB, cur.at[2], "below")
    c_do1 = copy(DO1, cur.at[0], "partner")
    c_uo1 = copy(UO1, cur.at[1], "partner")
    c_uao = copy(UAO, fresh_ref.at[0], "partner")
    c_ul1 = copy(UL1, fresh_ref.at[0], "over")
    c_fl1 = copy(FL1, fresh_ref.at[1], "over")
    c_ru = copy(RU, fresh_ref.at[0], "above", uout_ref.at[0])
    c_rf = copy(RF, fresh_ref.at[1], "above", fout_ref.at[0])
    c_zlr = copy_tiles(ZLR, ztiles.at[0], "over")
    c_zl = copy_tiles(ZL, zbufs.at[ZLR], "below")
    c_zlo = copy_tiles(ZLO, zbufs.at[ZL], "partner")
    c_za = copy_tiles(ZA, ztiles.at[1], "below")
    c_zao = copy_tiles(ZAO, zbufs.at[ZA], "partner")
    c_zl1 = copy_tiles(ZL1, zbufs.at[ZA], "over")
    c_zl1o = copy_tiles(ZL1O, zbufs.at[ZL1], "partner")

    c_do.start()
    pl.when(odd)(c_e.start)

    pl.when(odd_over)(c_ulr.start)
    c_uo.start()
    c_eo.start()
    fill_own(d_ref.at[1])

    def ready():
        c_do.wait_recv()
        fill_other(bufs.at[DO])

    def send(k):
        send_factor(k)
        pl.when(jnp.logical_and(odd_over, k == 1))(c_flr.start)

        @pl.when(jnp.logical_and(odd_under, k == 1))
        def _():
            c_ulr.wait_recv()
            c_ulf.start()

    invert(s_ref, tile_ref, fac_ref, col_ref, ready, send, lambda k: None)

    @pl.when(odd_over)
    def _():
        pack(ztiles.at[0])
        for i in c_zlr:
            i.start()

    store_inverse()
    c_uo.wait_recv()
    left(
        u_ref.at[1], bufs.at[UO], f_ref.at[1], d_ref.at[0], f_ref.at[0], cur.at[0], cur.at[2], scaled_ref
    )
    c_eo.wait_recv()

    @pl.when(odd)
    def _():
        c_fb.start()
        full_ref[:half] = u_ref[0]
        full_ref[half:] = bufs[EO]
        right_block(cur.at[0])
        c_do1.start()
        fill_own(cur.at[0])

        def ready():
            c_do1.wait_recv()
            fill_other(bufs.at[DO1])
            dout_ref[0] = cur[0]

            @pl.when(odd_under)
            def _():
                for arriving, sent in zip(c_zlr, c_zl):
                    arriving.wait_recv()
                    sent.start()

        def after(k):
            @pl.when(jnp.logical_and(odd_under, k == 1))
            def _():
                c_flr.wait_recv()
                c_flf[0].start()

        invert(s_ref, tile_ref, fac_ref, col_ref, ready, lambda k: None, after)
        pack(ztiles.at[1])
        for n, i in enumerate(c_za):
            i.start()
            if n > 0:
                c_za[n - 1].wait_send()
        c_za[-1].wait_send()
        pl.when(odd_under)(c_flf[1].start)
        keep()
        c_ru.wait_recv()
        c_rf.wait_recv()

    @pl.when(even)
    def _():
        c_e.wait_recv()
        c_ex.start()
        c_ex.wait_recv()
        assemble(onward_ref, bufs.at[EB], bufs.at[EX])
        fresh_ref[0] = -dot3(scaled_ref[0], onward_ref[...])
        c_ru.start()
        c_uao.start()
        pl.when(even_right)(c_ul1.start)
        c_fb.wait_recv()
        fresh_ref[1] = bufs[FB] - dot3(scaled_ref[1], onward_ref[...])
        c_rf.start()
        pl.when(even_right)(c_fl1.start)
        cur[1] = u_ref[0]

        @pl.when(has_left)
        def _():
            receive(ZL, ZLO, c_zl, c_zlo)
            assemble(full_ref, u_ref.at[0], bufs.at[EO])
            ahead(ahead_ref)
            c_ulf.wait_recv()
            right(ahead_ref, bufs.at[UL], cur.at[0], cur.at[1])

        c_uo1.start()
        keep()
        c_uo1.wait_recv()
        assemble(full_ref, cur.at[1], bufs.at[UO1])
        uout_ref[0] = cur[1]
        c_uao.wait_recv()

        @pl.when(has_left)
        def _():
            c_flf[0].wait_recv()
            right_source(ahead_ref, bufs.at[FL, top], cur.at[2, top])

        receive(ZA, ZAO, c_za, c_zao, c_zl1, even_right)
        left(
            fresh_ref.at[0], bufs.at[UAO], fresh_ref.at[1], cur.at[0], cur.at[2], dout_ref.at[0], fout_ref.at[0]
        )

    @pl.when(even_left)
    def _():
        receive(ZL1, ZL1O, c_zl1, c_zl1o)
        ahead(onward_ref)
        c_ul1.wait_recv()
        right(onward_ref, bufs.at[UL1], dout_ref.at[0], uout_ref.at[0])
        c_fl1.wait_recv()
        right_source(onward_ref, bufs.at[FL1], fout_ref.at[0])
        c_flf[1].wait_recv()
        right_source(ahead_ref, bufs.at[FL, low], fout_ref.at[0, low])

    def drained(condition, copies):
        @pl.when(condition)
        def _():
            for i in copies:
                i.wait_send()

    for i in (c_do, c_uo, c_eo):
        i.wait_send()
    drained(odd_over, [c_ulr, c_flr] + c_zlr)
    drained(odd_under, [c_ulf] + c_flf + c_zl)
    drained(even_left, c_zlo)
    drained(even, [copy_factor(k, c) for k in range(blocks) for c in range(k, blocks)])
    drained(odd, [c_e, c_fb, c_do1])
    drained(even, [c_ex, c_ru, c_rf, c_uao, c_uo1] + c_zao)
    drained(even_right, [c_ul1, c_fl1] + c_zl1)
    drained(even_left, c_zl1o)


SLOTS = 18
DO, UO, EO, EB, EX, ULR, FLR, UL, FL, FB, DO1, UO1, UAO, UL1, FL1, FL2, RU, RF = range(SLOTS)
ZSLOTS = 7
ZLR, ZL, ZLO, ZA, ZAO, ZL1, ZL1O = range(ZSLOTS)
ZTILES = 4


def body(tm_size, diagonal_blocks, upper_blocks, right_sides):
    shape = diagonal_blocks.shape
    half, size = shape[1], shape[2]
    tile, blocks = half // 2, size // TILE
    whole = pl.BlockSpec(memory_space=pltpu.VMEM)
    return pl.pallas_call(
        functools.partial(kernel, tm_size),
        out_shape=[jax.ShapeDtypeStruct(shape, F32)] * 3,
        in_specs=[whole] * 3,
        out_specs=[whole] * 3,
        scratch_shapes=[
            pltpu.VMEM((size, size), F32),
            pltpu.VMEM((TILE, TILE), F32),
            pltpu.VMEM((blocks, blocks, TILE, TILE), F32),
            pltpu.VMEM((blocks - 1, TILE, TILE), F32),
            pltpu.VMEM((size, size), F32),
            pltpu.VMEM((size, size), F32),
            pltpu.VMEM((size, size), F32),
            pltpu.VMEM((size, size), F32),
            pltpu.VMEM((3, half, size), F32),
            pltpu.VMEM((2, half, size), F32),
            pltpu.VMEM((2, half, size), F32),
            pltpu.VMEM((2, ZTILES, tile + PANEL, tile), F32),
            pltpu.VMEM((FL2, half, size), F32),
            pltpu.VMEM((ZSLOTS, ZTILES, tile + PANEL, tile), F32),
            pltpu.VMEM((blocks, blocks, TILE, TILE), F32),
            pltpu.SemaphoreType.DMA((SLOTS,)),
            pltpu.SemaphoreType.DMA((SLOTS,)),
            pltpu.SemaphoreType.DMA((ZSLOTS * ZTILES,)),
            pltpu.SemaphoreType.DMA((ZSLOTS * ZTILES,)),
            pltpu.SemaphoreType.DMA((blocks * blocks,)),
            pltpu.SemaphoreType.DMA((blocks * blocks,)),
        ],
        compiler_params=pltpu.CompilerParams(
            vmem_limit_bytes=50 * 2**20, collective_id=0, has_side_effects=True
        ),
        name="reduce_levels",
    )(diagonal_blocks, upper_blocks, right_sides)


def solution(mesh):
    placed = (P("tm", "col", None),) * 3
    return jax.shard_map(
        functools.partial(body, mesh.shape["tm"]),
        mesh=mesh,
        in_specs=placed,
        out_specs=placed,
        check_vma=False,
    )
```
